128 devices in a mesh: rep: 16 (over x, z), grp: 8 (over y, core).
Axes of the slice: x: 4, y: 4, z: 4, core: 2. Of those that a mesh axis runs over, the one named last changes fastest.
Arguments:
- inputs: bfloat16 [2, 262144, 1152], P(None, ('rep', 'grp')), may hold values from -6 to 6
- out_grads: bfloat16 [2, 262144, 1152], P(None, ('rep', 'grp')), may hold values from -6 to 6
- weights: bfloat16 [2, 1152, 1152], P(None, 'grp'), may hold values from -3 to 3
- biases: bfloat16 [2, 1152], P(None, 'grp'), may hold values from -3 to 3
- errors: float32 [16, 2, 1152, 1152], P('rep', None, 'grp'), may hold values from -6 to 6
- momenta: float32 [2, 1152, 1152], P(None, 'grp'), may hold values from -3 to 3
- bias_momenta: float32 [2, 1152], P(None, 'grp'), may hold values from -3 to 3
- q_start: float32 [2, 1152, 32], replicated, may hold values from -6 to 6
Outputs:
- new_weights: bfloat16 [2, 1152, 1152], replicated
- new_biases: bfloat16 [2, 1152], replicated
- new_errors: float32 [16, 2, 1152, 1152], P('rep', None, 'grp')
- new_momenta: float32 [2, 1152, 1152], P(None, 'grp')
- new_bias_momenta: float32 [2, 1152], P(None, 'grp')
The draws below stay inside these ranges and needn't reach their ends.
All inputs are finite; a program needn't handle non-finite values.
Results may differ from the reference program's by a relative error of at most 0.0045.
Values may be sent and summed in bfloat16 or wider, within the bound.
No kernel may reach another device: no remote copies, remote signals or barrier semaphores. Data moves between devices by JAX's collectives and lax.ppermute only.
A program may use at most 256 MiB of HBM per device.

```python
import jax
import jax.numpy as jnp
from jax import lax

D = 1152
RANK = 32
LAYERS = 2
ROUNDS = 2
NS_STEPS = 5
TOK_DEV = 2048
REPS = 16
TOKENS = 262144
N_GRP = 8


def steps_of(rng, dims, cuts, low, top_value):
    factor_of, own = 1.0, jax.random.fold_in(rng, 6)
    for dim, blocks in cuts:
        heights = jnp.exp(jax.random.uniform(jax.random.fold_in(own, dim), (blocks,), jnp.float32, low / len(cuts), top_value / len(cuts)))
        factor_of = factor_of * jnp.repeat(heights, dims[dim] // blocks).reshape([-1 if axis == dim else 1 for axis in range(len(dims))])
    return factor_of


def gaussian(rng, extent, width, reach, pieces=(), kind=jnp.bfloat16):
    result = jax.random.normal(rng, extent, jnp.float32) * width
    if len(pieces) > 0:
        result = steps_of(rng, extent, pieces, -0.22, 0.18) * result
    return jnp.clip(result, min=-reach, max=reach).astype(kind)


def setup_inputs(seed: int = 0) -> dict:
    streams_of = jax.random.split(jax.random.key(seed), 9)
    return {
        "inputs": gaussian(streams_of[0], (LAYERS, TOKENS, D), 1.0, 6.0, ((1, 128),)),
        "out_grads": gaussian(streams_of[1], (LAYERS, TOKENS, D), 1.0, 6.0, ((1, 128),)),
        "weights": gaussian(streams_of[2], (LAYERS, D, D), 0.5, 3.0, ((1, 8),)),
        "biases": gaussian(streams_of[3], (LAYERS, D), 0.5, 3.0, ((1, 8),)),
        "errors": gaussian(streams_of[4], (REPS, LAYERS, D, D), 1.0, 6.0, ((0, 16), (2, 8)), jnp.float32),
        "momenta": gaussian(streams_of[5], (LAYERS, D, D), 0.5, 3.0, ((1, 8),), jnp.float32),
        "bias_momenta": gaussian(streams_of[6], (LAYERS, D), 0.5, 3.0, ((1, 8),), jnp.float32),
        "q_start": gaussian(streams_of[7], (LAYERS, D, RANK), 1.0, 6.0, (), jnp.float32),
    }


HIGH = lax.Precision.HIGHEST

def orthonormal(p_sum, gram):
    fro = jnp.sqrt(lax.optimization_barrier(jnp.sum(gram * gram, axis=(1, 2)))) + 1e-06
    scaled = gram / fro[:, None, None]
    eye = jnp.eye(gram.shape[-1], dtype=jnp.float32)
    ymat = scaled
    zmat = jnp.broadcast_to(eye, gram.shape)
    for step in range(NS_STEPS):
        tmat = 1.5 * eye - 0.5 * jnp.einsum('lab,lbc->lac', zmat, ymat, precision=HIGH)
        ymat = jnp.einsum('lab,lbc->lac', ymat, tmat, precision=HIGH)
        zmat = jnp.einsum('lab,lbc->lac', tmat, zmat, precision=HIGH)
    phat = jnp.einsum('lrk,lkj->lrj', p_sum, zmat, precision=HIGH)
    return phat / jnp.sqrt(fro)[:, None, None]

def reference(inputs, out_grads, weights, biases, errors, momenta, bias_momenta, q_start):
    rep_tok = TOK_DEV * N_GRP
    scale = float(TOK_DEV) ** (-0.5)

    def replica(index):
        start = (index * rep_tok).astype(jnp.int32)
        xs = lax.dynamic_slice_in_dim(inputs, start, rep_tok, 1)
        ys = lax.dynamic_slice_in_dim(out_grads, start, rep_tok, 1)
        grads = [jnp.dot(xs[l].T, ys[l], preferred_element_type=jnp.float32) for l in range(LAYERS)]
        return jnp.stack(grads) * scale
    grad = lax.map(replica, jnp.arange(REPS, dtype=jnp.int32))
    merged = grad + errors
    bias_grad = lax.optimization_barrier(jnp.sum(out_grads, axis=1, dtype=jnp.float32)) * (scale / REPS)
    qmat = q_start
    phat = None
    for rnd in range(ROUNDS):
        p_sum = jnp.einsum('xlde,lek->ldk', merged, qmat, precision=HIGH)
        gram = jnp.einsum('ldk,ldj->lkj', p_sum, p_sum, precision=HIGH)
        phat = orthonormal(p_sum, gram)
        qmat = jnp.einsum('xlde,ldk->lek', merged, phat, precision=HIGH)
    approx = jnp.einsum('ldk,lek->lde', phat, qmat, precision=HIGH) / REPS
    new_errors = merged - approx[None]
    new_momenta = 0.9 * momenta + approx
    new_weights = (weights.astype(jnp.float32) - 0.5 * new_momenta).astype(jnp.bfloat16)
    new_bias_momenta = 0.9 * bias_momenta + bias_grad
    new_biases = (biases.astype(jnp.float32) - 0.5 * new_bias_momenta).astype(jnp.bfloat16)
    return (new_weights, new_biases, new_errors, new_momenta, new_bias_momenta)
```

```python
import jax
import jax.numpy as jnp
from jax import lax
from jax.experimental import pallas as pl
from jax.experimental.pallas import tpu as pltpu
from jax.sharding import Mesh
from jax.sharding import PartitionSpec as P

ROUNDS = 2
NS_STEPS = 5
HIGH = lax.Precision.HIGHEST
BF = jnp.bfloat16
F32 = jnp.float32


def ring(count, step):
    return [(i, (i + step) % count) for i in range(count)]


def pick(stack, index, axis=0):
    return lax.dynamic_index_in_dim(stack, index, axis, keepdims=False)


def hi_lo(row):
    high = row.astype(BF)
    low = (row - high.astype(F32)).astype(BF)
    return jnp.concatenate([high[None], low[None], jnp.zeros((6, row.shape[0]), BF)], 0)


def from_hi_lo(rows):
    return rows[0].astype(F32) + rows[1].astype(F32)


def paired(parts):
    return (parts[0] + parts[2]) + (parts[1] + parts[3])


def split3(value):
    one = value.astype(BF)
    rest = value - one.astype(F32)
    two = rest.astype(BF)
    three = (rest - two.astype(F32)).astype(BF)
    return jnp.concatenate([one, two, three], 0)


def by_three(left, right, dims):
    rank = left.shape[0]
    out = lax.dot_general(split3(left), right, dims, preferred_element_type=F32)
    return out[:rank] + out[rank : 2 * rank] + out[2 * rank :]


def inverse_root(gram):
    fro = jnp.sqrt(jnp.sum(gram * gram)) + 1e-06
    eye = jnp.eye(gram.shape[-1], dtype=F32)
    ymat = gram / fro
    zmat = eye
    for _ in range(NS_STEPS):
        tmat = 1.5 * eye - 0.5 * jnp.dot(zmat, ymat, precision=HIGH)
        ymat = jnp.dot(ymat, tmat, precision=HIGH)
        zmat = jnp.dot(tmat, zmat, precision=HIGH)
    return zmat, jnp.sqrt(fro)


def weights_kernel(reps, place_ref, old_ref, left_ref, right_ref, out_ref):
    for layer in range(out_ref.shape[0]):
        approx = jnp.dot(
            left_ref[layer], right_ref[layer], precision=HIGH, preferred_element_type=F32
        ) / reps
        out_ref[layer] = (old_ref[0, 0, layer].astype(F32) - 0.5 * approx).astype(BF)


def new_weights_of(old, left, right, place, reps):
    _, ys, layers, rows, width = old.shape
    rank = left.shape[-1]
    import functools

    return pl.pallas_call(
        functools.partial(weights_kernel, reps),
        out_shape=jax.ShapeDtypeStruct((layers, 2 * ys * rows, width), BF),
        grid_spec=pltpu.PrefetchScalarGridSpec(
            num_scalar_prefetch=1,
            grid=(2 * ys,),
            in_specs=[
                pl.BlockSpec(
                    (1, 1, layers, rows, width),
                    lambda i, place: (place[i], place[2 * ys + i], 0, 0, 0),
                ),
                pl.BlockSpec((layers, rows, rank), lambda i, place: (0, i, 0)),
                pl.BlockSpec((layers, rank, width), lambda i, place: (0, 0, 0)),
            ],
            out_specs=pl.BlockSpec((layers, rows, width), lambda i, place: (0, i, 0)),
        ),
        name="new_weights",
    )(place, old, left, right)


def body(inputs, out_grads, weights, biases, errors, momenta, bias_momenta, q_start):
    layers, tok, width = inputs.shape
    cores = lax.axis_size("core")
    ys = lax.axis_size("y")
    xs = lax.axis_size("x")
    reps = xs * lax.axis_size("z")
    rows = width // (cores * ys)
    rank = q_start.shape[-1]
    scale = float(tok) ** (-0.5)
    core, ypos, xpos = lax.axis_index("core"), lax.axis_index("y"), lax.axis_index("x")

    def swap(value):
        return lax.ppermute(value, "core", ring(cores, 1))

    def from_back(value, axis, step):
        return lax.ppermute(value, axis, ring(4, step))

    def everyone(value, axis):
        return [value] + [from_back(value, axis, k) for k in (1, 2, 3)]

    def natural(parts, position):
        stack = jnp.stack(parts)
        return [pick(stack, (position - j) % 4) for j in range(4)]

    old_w = (weights.astype(F32) - 0.45 * momenta).astype(BF)
    old_b = biases.astype(F32) - 0.45 * bias_momenta
    old_b = jnp.pad(old_b, ((0, 0), (0, 256 - rows)))

    merged = []
    for layer in range(layers):
        part = jnp.einsum(
            "tr,te->re", inputs[layer], out_grads[layer], preferred_element_type=F32
        ).reshape(ys, cores, rows, width)
        got = swap(pick(part, 1 - core, 1).astype(BF))
        chip = pick(part, core, 1) + got.astype(F32)
        own = pick(chip, ypos)
        for k in (1, 3, 2):
            own = own + from_back(pick(chip, (ypos + k) % 4).astype(BF), "y", k).astype(F32)
        merged.append(own * scale + errors[0, layer])
    merged = jnp.stack(merged)
    col_sums = jnp.sum(out_grads, axis=1, dtype=F32)

    got = swap(
        jnp.concatenate([pick(merged, 1 - core).astype(BF), hi_lo(pick(col_sums, 1 - core))], 0)
    )
    both = jnp.stack([pick(merged, core), got[:rows].astype(F32)]).reshape(4, rows // 2, width)
    bias = pick(col_sums, core) + from_hi_lo(got[rows:])
    bias_rows = hi_lo(bias)
    half = rows // 2

    def loaded(main):
        return jnp.concatenate([main.astype(BF), bias_rows], 0)

    parts = [loaded(pick(both, xpos))] + [
        from_back(loaded(pick(both, (xpos + k) % 4)), "x", k) for k in (1, 2, 3)
    ]
    main = paired([p[:half].astype(F32) for p in parts])
    bias = paired([from_hi_lo(p[half:]) for p in parts])
    bias_rows = hi_lo(bias)
    parts = everyone(loaded(main), "z")
    main = paired([p[:half].astype(F32) for p in parts]).astype(BF)
    bias = paired([from_hi_lo(p[half:]) for p in parts])
    total = jnp.concatenate(natural(everyone(main, "x"), xpos), 0)

    q = pick(q_start, core).T
    for rnd in range(ROUNDS):
        p = by_three(q, total, (((1,), (1,)), ((), ())))
        gram = lax.dot_general(p, p, (((1,), (1,)), ((), ())), precision=HIGH)
        u = by_three(p, total, (((1,), (0,)), ((), ())))
        packed = jnp.concatenate([u, jnp.pad(gram, ((0, 0), (0, 128 - rank)))], 1)
        if rnd == 0:
            last = jnp.concatenate([bias[None], jnp.zeros((1, 128), F32)], 1)
            packed = jnp.concatenate([packed, jnp.pad(last, ((0, 7), (0, 0)))], 0)
            parts = everyone(packed, "y")
        else:
            packed = jnp.concatenate([packed, jnp.pad(p, ((0, 0), (0, 96)))], 1)
            parts = everyone(packed, "y")
        summed = paired([part[:, : width + 128] for part in parts])
        zmat, root = inverse_root(summed[:rank, width : width + rank])
        q = lax.dot_general(zmat, summed[:rank, :width], (((0,), (0,)), ((), ())), precision=HIGH) / root
        if rnd == 0:
            bias = summed[rank, :width]
    p_all = natural([part[:, width + 128 : width + 128 + 2 * rows] for part in parts], ypos)
    phat = lax.dot_general(
        zmat, jnp.concatenate(p_all, 1), (((0,), (0,)), ((), ())), precision=HIGH
    ) / root

    packed = jnp.concatenate(
        [q, phat, jnp.pad(bias[None], ((0, 7), (0, 0)))], 0
    )
    other = swap(packed)
    pair = jnp.stack([packed, other])
    pair = jnp.stack([pick(pair, core), pick(pair, 1 - core)])
    q = pair[:, :rank]
    bias = pair[:, 2 * rank]
    phat = pair[:, rank : 2 * rank].reshape(layers, rank, ys, cores, rows)
    phat = jnp.stack([phat[0], phat[1, :, :, ::-1]])
    phat = phat.transpose(0, 2, 3, 4, 1).reshape(layers, width, rank)

    grp = ypos * cores + core
    approx = jnp.einsum(
        "lrk,lke->lre",
        lax.dynamic_slice_in_dim(phat, grp * rows, rows, 1),
        q,
        precision=HIGH,
    ) / reps
    new_errors = (merged - approx)[None]
    new_momenta = 0.9 * momenta + approx
    bias_grad = bias * (scale / reps)
    new_bias_momenta = 0.9 * bias_momenta + lax.dynamic_slice_in_dim(bias_grad, grp * rows, rows, 1)

    mine = everyone(old_w, "y")
    mine = jnp.stack(mine)
    old = jnp.stack([mine, swap(mine)])
    j = jnp.arange(ys * cores)
    place = jnp.concatenate([(j % cores) ^ core, (ypos - j // cores) % 4]).astype(jnp.int32)
    new_weights = new_weights_of(old, phat, q, place, reps)

    b_own = jnp.stack(natural(everyone(old_b, "y"), ypos))
    b_both = jnp.stack([b_own, swap(b_own)])
    b_all = jnp.stack([pick(b_both, core), pick(b_both, 1 - core)])[..., :rows]
    b_all = b_all.transpose(2, 1, 0, 3).reshape(layers, width)
    new_biases = (b_all - 0.5 * bias_grad).astype(BF)
    return (new_weights, new_biases, new_errors, new_momenta, new_bias_momenta)


def solution(mesh):
    split = Mesh(mesh.devices.reshape(4, 4, 4, 2), ("x", "z", "y", "core"))
    rep, grp = ("x", "z"), ("y", "core")
    placed = (
        P(None, rep + grp, None),
        P(None, rep + grp, None),
        P(None, grp, None),
        P(None, grp),
        P(rep, None, grp, None),
        P(None, grp, None),
        P(None, grp),
        P(),
    )
    return jax.shard_map(
        body,
        mesh=split,
        in_specs=placed,
        out_specs=(P(), P(), P(rep, None, grp, None), P(None, grp, None), P(None, grp)),
        check_vma=False,
    )
```

```python
import functools

import jax
import jax.numpy as jnp
from jax import lax
from jax.experimental import pallas as pl
from jax.experimental.pallas import tpu as pltpu
from jax.sharding import Mesh
from jax.sharding import PartitionSpec as P


ROUNDS = 2
NS_STEPS = 5
HIGH = lax.Precision.HIGHEST
BF = jnp.bfloat16
F32 = jnp.float32


def ring(count, step):
    return [(i, (i + step) % count) for i in range(count)]


def pick(stack, index, axis=0):
    return lax.dynamic_index_in_dim(stack, index, axis, keepdims=False)


def hi_lo(row):
    high = row.astype(BF)
    low = (row - high.astype(F32)).astype(BF)
    return jnp.concatenate([high[None], low[None], jnp.zeros((6, row.shape[0]), BF)], 0)


def from_hi_lo(rows):
    return rows[0].astype(F32) + rows[1].astype(F32)


def paired(parts):
    return (parts[0] + parts[2]) + (parts[1] + parts[3])


def split3(value):
    one = value.astype(BF)
    rest = value - one.astype(F32)
    two = rest.astype(BF)
    three = (rest - two.astype(F32)).astype(BF)
    return jnp.concatenate([one, two, three], 0)


def by_three(left, right, dims):
    rank = left.shape[0]
    out = lax.dot_general(split3(left), right, dims, preferred_element_type=F32)
    return out[:rank] + out[rank : 2 * rank] + out[2 * rank :]


def inverse_root(gram):
    fro = jnp.sqrt(jnp.sum(gram * gram)) + 1e-06
    eye = jnp.eye(gram.shape[-1], dtype=F32)
    ymat = gram / fro
    zmat = eye
    for _ in range(NS_STEPS):
        tmat = 1.5 * eye - 0.5 * jnp.dot(zmat, ymat, precision=HIGH)
        ymat = jnp.dot(ymat, tmat, precision=HIGH)
        zmat = jnp.dot(tmat, zmat, precision=HIGH)
    return zmat, jnp.sqrt(fro)


def products(left, right):
    l1 = left.astype(BF)
    rest = left - l1.astype(F32)
    l2 = rest.astype(BF)
    l3 = (rest - l2.astype(F32)).astype(BF)
    r1 = right.astype(BF)
    rest = right - r1.astype(F32)
    r2 = rest.astype(BF)
    r3 = (rest - r2.astype(F32)).astype(BF)
    return (
        jnp.concatenate([l1, l1, l2, l1, l2, l3], -2),
        jnp.concatenate([r1, r2, r1, r3, r2, r1], -2),
    )


def final_kernel(reps, ys, place_ref, *refs):
    mine, theirs = refs[0:2], refs[2:4]
    left, right = refs[4:6], refs[6]
    merged_ref, momenta_ref, out_ref, errors_ref, new_momenta_ref = refs[7:]
    rows = out_ref.shape[1]
    step = pl.program_id(0)
    for layer in range(out_ref.shape[0]):
        approx = lax.dot_general(
            left[layer][...],
            right[layer],
            (((0,), (0,)), ((), ())),
            preferred_element_type=F32,
        )[:rows] * (1.0 / reps)

        @pl.when(step < ys)
        def _():
            out_ref[layer] = (mine[layer][0, :rows].astype(F32) - 0.5 * approx).astype(BF)

        @pl.when(step >= ys)
        def _():
            out_ref[layer] = (theirs[layer][0, :rows].astype(F32) - 0.5 * approx).astype(BF)

        @pl.when(step == 0)
        def _():
            errors_ref[layer] = merged_ref[layer] - approx
            new_momenta_ref[layer] = 0.9 * momenta_ref[layer] + approx


def finish(mine, theirs, left, right, merged, momenta, place, reps):
    ys, held, width = mine[0].shape
    rows = merged.shape[1]
    layers, deep, _ = right.shape
    old = lambda spot: pl.BlockSpec((1, held, width), spot)
    whole = lambda *shape: pl.BlockSpec(shape, lambda i, place: (0,) * len(shape))
    return pl.pallas_call(
        functools.partial(final_kernel, reps, ys),
        out_shape=(
            jax.ShapeDtypeStruct((layers, 2 * ys * rows, width), BF),
            jax.ShapeDtypeStruct((layers, rows, width), F32),
            jax.ShapeDtypeStruct((layers, rows, width), F32),
        ),
        grid_spec=pltpu.PrefetchScalarGridSpec(
            num_scalar_prefetch=1,
            grid=(2 * ys,),
            in_specs=[old(lambda i, place: (jnp.minimum(i, ys - 1), 0, 0))] * layers
            + [old(lambda i, place: (jnp.maximum(i - ys, 0), 0, 0))] * layers
            + [
                pl.BlockSpec((deep, 256), lambda i, place: (0, place[2 * ys + i])),
                pl.BlockSpec((deep, 256), lambda i, place: (0, place[4 * ys + i])),
                whole(layers, deep, width),
                whole(layers, rows, width),
                whole(layers, rows, width),
            ],
            out_specs=[
                pl.BlockSpec((layers, rows, width), lambda i, place: (0, place[i], 0)),
                whole(layers, rows, width),
                whole(layers, rows, width),
            ],
        ),
        name="finish",
    )(place, *mine, *theirs, *left, right, merged, momenta)


def body(inputs, out_grads, weights, biases, errors, momenta, bias_momenta, q_start):
    layers, tok, width = inputs.shape
    cores = lax.axis_size("core")
    ys = lax.axis_size("y")
    xs = lax.axis_size("x")
    reps = xs * lax.axis_size("z")
    rows = width // (cores * ys)
    rank = q_start.shape[-1]
    scale = float(tok) ** (-0.5)
    core, ypos, xpos = lax.axis_index("core"), lax.axis_index("y"), lax.axis_index("x")

    def swap(value):
        return lax.ppermute(value, "core", ring(cores, 1))

    def from_back(value, axis, step):
        return lax.ppermute(value, axis, ring(4, step))

    def everyone(value, axis):
        return [value] + [from_back(value, axis, k) for k in (1, 2, 3)]

    def natural(parts, position):
        ordered = []
        for j in range(4):
            value = parts[-j % 4]
            for spot in (1, 2, 3):
                value = jnp.where(position == spot, parts[(spot - j) % 4], value)
            ordered.append(value)
        return ordered

    def old_of(layer, after=None):
        w, m = weights[layer], momenta[layer]
        if after is not None:
            w, m, _ = lax.optimization_barrier((w, m, after))
        shard = (w.astype(F32) - 0.45 * m).astype(BF)
        row = biases[layer].astype(F32) - 0.45 * bias_momenta[layer]
        shard = jnp.concatenate([shard, hi_lo(jnp.pad(row, (0, width - rows)))], 0)
        parts = everyone(shard, "y")
        mine = jnp.stack(parts)
        theirs = swap(mine)
        return mine, theirs

    mine0, theirs0 = old_of(0)

    def chip_blocks(layer, after=None):
        x, y = inputs, out_grads
        if after is not None:
            x, y, _ = lax.optimization_barrier((x, y, after))
        part = jnp.einsum("tr,te->re", x[layer], y[layer], preferred_element_type=F32)
        part = lax.optimization_barrier(part).reshape(ys * cores, rows, width)
        got = swap(
            pick(part.reshape(ys, cores, rows, width), 1 - core, 1).astype(BF)
        )
        blocks = []
        for k in range(4):
            there = (ypos + k) % 4
            blocks.append(pick(part, there * cores + core) + pick(got, there).astype(F32))
        return blocks[0], [b.astype(BF) for b in blocks[1:]]

    def merge(layer, own, blocks):
        for k in (1, 3, 2):
            block = from_back(blocks[k - 1], "y", k)
            own = own + block.astype(F32)
        return own * scale + errors[0, layer]

    own0, blocks0 = chip_blocks(0)
    own1, blocks1 = chip_blocks(1, blocks0)
    merged = jnp.stack([merge(0, own0, blocks0), merge(1, own1, blocks1)])
    col_sums = jnp.sum(out_grads, axis=1, dtype=F32)

    got = swap(
        jnp.concatenate([pick(merged, 1 - core).astype(BF), hi_lo(pick(col_sums, 1 - core))], 0)
    )
    mine1, theirs1 = old_of(1)
    both = jnp.stack([pick(merged, core), got[:rows].astype(F32)]).reshape(4, rows // 2, width)
    bias = pick(col_sums, core) + from_hi_lo(got[rows:])
    bias_rows = hi_lo(bias)
    half = rows // 2

    def loaded(main):
        return jnp.concatenate([main.astype(BF), bias_rows], 0)

    parts = [loaded(pick(both, xpos))]
    for k in (1, 2, 3):
        block = loaded(pick(both, (xpos + k) % 4))
        parts.append(from_back(block, "x", k))
    main = paired([p[:half].astype(F32) for p in parts])
    bias = paired([from_hi_lo(p[half:]) for p in parts])
    bias_rows = hi_lo(bias)
    parts = everyone(loaded(main), "z")
    main = paired([p[:half].astype(F32) for p in parts]).astype(BF)
    bias = paired([from_hi_lo(p[half:]) for p in parts])
    parts = everyone(main, "x")
    quarter = natural(parts, xpos)
    gap = jnp.zeros((256 - rows, width), BF)
    total = jnp.concatenate(quarter[:2] + [gap] + quarter[2:] + [gap], 0)

    q = pick(q_start, core).T
    for rnd in range(ROUNDS):
        p = by_three(q, total, (((1,), (1,)), ((), ())))
        gram = lax.dot_general(p, p, (((1,), (1,)), ((), ())), precision=HIGH)
        u = by_three(p, total, (((1,), (0,)), ((), ())))
        packed = jnp.concatenate([u, jnp.pad(gram, ((0, 0), (0, 128 - rank)))], 1)
        if rnd == 0:
            last = jnp.concatenate([bias[None], jnp.zeros((1, 128), F32)], 1)
            packed = jnp.concatenate([packed, jnp.pad(last, ((0, 7), (0, 0)))], 0)
        else:
            packed = jnp.concatenate([packed, p], 1)
        parts = everyone(packed, "y")
        summed = paired([part[:, : width + 128] for part in parts])
        zmat, root = inverse_root(summed[:rank, width : width + rank])
        q = lax.dot_general(zmat, summed[:rank, :width], (((0,), (0,)), ((), ())), precision=HIGH) / root
        if rnd == 0:
            bias = summed[rank, :width]
    p_all = jnp.concatenate(natural([part[:, width + 128 :] for part in parts], ypos), 1)
    phat = lax.dot_general(zmat, p_all, (((0,), (0,)), ((), ())), precision=HIGH) / root

    last = jnp.concatenate([bias[None], jnp.zeros((1, phat.shape[1]), F32)], 1)
    packed = jnp.concatenate(
        [jnp.concatenate([q, phat], 1), jnp.pad(last, ((0, 7), (0, 0)))], 0
    )
    other = swap(packed)
    pair = [jnp.where(core == layer, packed, other) for layer in range(layers)]
    bias = jnp.stack([p[rank, :width] for p in pair])
    factors = [products(p[:rank, width:], p[:rank, :width]) for p in pair]

    grp = ypos * cores + core
    i = jnp.arange(ys * cores)
    back, side = i % ys, core ^ (i // ys)
    where = ((ypos - back) % 4) * cores
    place = jnp.concatenate([where + side, where + side, where + (side ^ 1)]).astype(jnp.int32)
    new_weights, new_errors, new_momenta = finish(
        [mine0, mine1],
        [theirs0, theirs1],
        [f[0] for f in factors],
        jnp.stack([f[1] for f in factors]),
        merged,
        momenta,
        place,
        reps,
    )

    bias_grad = bias * (scale / reps)
    new_bias_momenta = 0.9 * bias_momenta + lax.dynamic_slice_in_dim(bias_grad, grp * rows, rows, 1)
    b_all = []
    for mine, theirs in ((mine0, theirs0), (mine1, theirs1)):
        both = []
        for stack in (mine, theirs):
            pieces = stack[:, rows : rows + 2, :rows].astype(F32)
            both.append(jnp.stack(natural(list(pieces[:, 0] + pieces[:, 1]), ypos)))
        even = jnp.where(core == 0, both[0], both[1])
        odd = jnp.where(core == 0, both[1], both[0])
        b_all.append(jnp.stack([even, odd], 1).reshape(width))
    b_all = jnp.stack(b_all)
    new_biases = (b_all - 0.5 * bias_grad).astype(BF)
    return (new_weights, new_biases, new_errors[None], new_momenta, new_bias_momenta)


def solution(mesh):
    split = Mesh(mesh.devices.reshape(4, 4, 4, 2), ("x", "z", "y", "core"))
    rep, grp = ("x", "z"), ("y", "core")
    placed = (
        P(None, rep + grp, None),
        P(None, rep + grp, None),
        P(None, grp, None),
        P(None, grp),
        P(rep, None, grp, None),
        P(None, grp, None),
        P(None, grp),
        P(),
    )

    return jax.shard_map(
        body,
        mesh=split,
        in_specs=placed,
        out_specs=(P(), P(), P(rep, None, grp, None), P(None, grp, None), P(None, grp)),
        check_vma=False,
    )
```

```python
import jax
import jax.numpy as jnp
from jax import lax
from jax.sharding import Mesh
from jax.sharding import PartitionSpec as P


ROUNDS = 2
NS_STEPS = 5
HIGH = lax.Precision.HIGHEST
BF = jnp.bfloat16
F32 = jnp.float32


def ring(count, step):
    return [(i, (i + step) % count) for i in range(count)]


def pick(stack, index, axis=0):
    return lax.dynamic_index_in_dim(stack, index, axis, keepdims=False)


def hi_lo(row):
    high = row.astype(BF)
    low = (row - high.astype(F32)).astype(BF)
    return jnp.concatenate([high[None], low[None], jnp.zeros((6, row.shape[0]), BF)], 0)


def from_hi_lo(rows):
    return rows[0].astype(F32) + rows[1].astype(F32)


def paired(parts):
    return (parts[0] + parts[1]) + (parts[2] + parts[3])


def split3(value):
    one = value.astype(BF)
    rest = value - one.astype(F32)
    two = rest.astype(BF)
    three = (rest - two.astype(F32)).astype(BF)
    return jnp.concatenate([one, two, three], 0)


def by_three(left, right, dims):
    rank = left.shape[0]
    out = lax.dot_general(split3(left), right, dims, preferred_element_type=F32)
    return out[:rank] + out[rank : 2 * rank] + out[2 * rank :]


def inverse_root(gram):
    fro = jnp.sqrt(jnp.sum(gram * gram)) + 1e-06
    eye = jnp.eye(gram.shape[-1], dtype=F32)
    ymat = gram / fro
    zmat = eye
    for _ in range(NS_STEPS):
        tmat = 1.5 * eye - 0.5 * jnp.dot(zmat, ymat, precision=HIGH)
        ymat = jnp.dot(ymat, tmat, precision=HIGH)
        zmat = jnp.dot(tmat, zmat, precision=HIGH)
    return zmat, jnp.sqrt(fro)


def products(left, right):
    l1 = left.astype(BF)
    rest = left - l1.astype(F32)
    l2 = rest.astype(BF)
    l3 = (rest - l2.astype(F32)).astype(BF)
    r1 = right.astype(BF)
    rest = right - r1.astype(F32)
    r2 = rest.astype(BF)
    r3 = (rest - r2.astype(F32)).astype(BF)
    return (
        jnp.concatenate([l1, l1, l2, l1, l2, l3], -2),
        jnp.concatenate([r1, r2, r1, r3, r2, r1], -2),
    )


def body(inputs, out_grads, weights, biases, errors, momenta, bias_momenta, q_start):
    layers, tok, width = inputs.shape
    cores = lax.axis_size("core")
    ys = lax.axis_size("y")
    xs = lax.axis_size("x")
    reps = xs * lax.axis_size("z")
    rows = width // (cores * ys)
    rank = q_start.shape[-1]
    scale = float(tok) ** (-0.5)
    core, ypos, xpos = lax.axis_index("core"), lax.axis_index("y"), lax.axis_index("x")

    def swap(value):
        return lax.ppermute(value, "core", ring(cores, 1))

    def trade(value, axis, k):
        return lax.ppermute(value, axis, [(i, i ^ k) for i in range(4)])

    def everyone(value, axis):
        return [value] + [trade(value, axis, k) for k in (1, 2, 3)]

    def natural(parts, position):
        ordered = []
        for j in range(4):
            value = parts[j]
            for spot in (1, 2, 3):
                value = jnp.where(position == spot, parts[spot ^ j], value)
            ordered.append(value)
        return ordered

    old_m = lax.optimization_barrier(momenta)
    old = (weights.astype(F32) - 0.45 * old_m).astype(BF)
    row_b, row_m = lax.optimization_barrier((biases, bias_momenta))
    two = jnp.stack([row_b, row_m.astype(BF)], 1)
    old = jnp.concatenate([old, jnp.pad(two, ((0, 0), (0, 6), (0, width - rows)))], 1)
    parts = everyone(old, "y")
    mine = jnp.stack(natural(parts, ypos))
    theirs = swap(mine)
    even, odd = jnp.where(core == 0, mine, theirs), jnp.where(core == 0, theirs, mine)
    old = jnp.stack([even, odd], 1)
    old_b = old[:, :, :, rows, :rows].astype(F32) - 0.45 * old[:, :, :, rows + 1, :rows].astype(F32)
    old_b = old_b.transpose(2, 0, 1, 3).reshape(layers, width)
    old = old[:, :, :, :rows].transpose(2, 0, 1, 3, 4).reshape(layers, width, width)
    old, old_b = lax.optimization_barrier((old, old_b))

    def chip_blocks(layer, after=None):
        x, y = inputs, out_grads
        if after is not None:
            x, y, _ = lax.optimization_barrier((x, y, after))
        part = jnp.einsum("tr,te->re", x[layer], y[layer], preferred_element_type=F32).astype(BF)
        part = lax.optimization_barrier(part).reshape(ys * cores, rows, width)
        got = swap(
            pick(part.reshape(ys, cores, rows, width), 1 - core, 1)
        )
        blocks = []
        for k in range(4):
            there = ypos ^ k
            blocks.append(pick(part, there * cores + core).astype(F32) + pick(got, there).astype(F32))
        return blocks[0], [b.astype(BF) for b in blocks[1:]]

    def merge(layer, own, blocks):
        for k in (1, 2, 3):
            block = trade(blocks[k - 1], "y", k)
            own = own + block.astype(F32)
        return own * scale + errors[0, layer]

    own0, blocks0 = chip_blocks(0)
    own1, blocks1 = chip_blocks(1, blocks0)
    merged = jnp.stack([merge(0, own0, blocks0), merge(1, own1, blocks1)])
    col_sums = jnp.sum(out_grads, axis=1, dtype=F32)

    got = swap(
        jnp.concatenate([pick(merged, 1 - core).astype(BF), hi_lo(pick(col_sums, 1 - core))], 0)
    )
    both = jnp.stack([pick(merged, core), got[:rows].astype(F32)]).reshape(4, rows // 2, width)
    bias = pick(col_sums, core) + from_hi_lo(got[rows:])
    bias_rows = hi_lo(bias)
    half = rows // 2

    def loaded(main):
        return jnp.concatenate([main.astype(BF), bias_rows], 0)

    parts = []
    for k in (1, 2, 3):
        block = loaded(pick(both, xpos ^ k))
        parts.append(trade(block, "x", k))
    main = paired([pick(both, xpos)] + [p[:half].astype(F32) for p in parts])
    bias = paired([from_hi_lo(p) for p in [bias_rows] + [p[half:] for p in parts]])
    bias_rows = hi_lo(bias)
    parts = everyone(loaded(main), "z")
    main = paired([p[:half].astype(F32) for p in parts]).astype(BF)
    bias = paired([from_hi_lo(p[half:]) for p in parts])
    parts = everyone(main, "x")
    quarter = natural(parts, xpos)
    total = jnp.concatenate(quarter, 0)

    q = pick(q_start, core).T
    for rnd in range(ROUNDS):
        p = by_three(q, total, (((1,), (1,)), ((), ())))
        gram = lax.dot_general(p, p, (((1,), (1,)), ((), ())), precision=HIGH)
        u = by_three(p, total, (((1,), (0,)), ((), ())))
        gram = jnp.pad(gram, ((0, 0), (0, 128 - rank)))
        if rnd == 0:
            wide = gram
        else:
            wide = jnp.concatenate([gram, jnp.pad(p, ((0, 0), (0, 384 - 2 * rows)))], 1)
        high = wide.astype(BF)
        packed = jnp.concatenate([u.astype(BF), high, (wide - high.astype(F32)).astype(BF)], 1)
        if rnd == 0:
            last = jnp.pad(hi_lo(bias), ((0, 0), (0, 256)))
            packed = jnp.concatenate([packed, last], 0)
        parts = everyone(packed, "y")
        span = wide.shape[1]
        wides = [
            part[:rank, width : width + span].astype(F32) + part[:rank, width + span :].astype(F32)
            for part in parts
        ]
        u = paired([part[:rank, :width].astype(F32) for part in parts])
        gram = paired([wide[:, :rank] for wide in wides])
        zmat, root = inverse_root(gram)
        q = lax.dot_general(zmat, u, (((0,), (0,)), ((), ())), precision=HIGH) / root
        if rnd == 0:
            bias = paired([from_hi_lo(part[rank:, :width]) for part in parts])
    p_all = natural([wide[:, 128 : 128 + 2 * rows] for wide in wides], ypos)
    p_all = jnp.concatenate(p_all, 1)
    phat = lax.dot_general(zmat, p_all, (((0,), (0,)), ((), ())), precision=HIGH) / root

    last = jnp.concatenate([bias[None], jnp.zeros((1, phat.shape[1]), F32)], 1)
    packed = jnp.concatenate(
        [jnp.concatenate([q, phat], 1), jnp.pad(last, ((0, 7), (0, 0)))], 0
    )
    other = swap(packed)
    pair = [jnp.where(core == layer, packed, other) for layer in range(layers)]
    bias = jnp.stack([p[rank, :width] for p in pair])
    q = jnp.stack([p[:rank, :width] for p in pair])
    phat = [p[:rank, width:].reshape(rank, ys, cores, rows) for p in pair]
    phat = jnp.stack([phat[0], phat[1][:, :, ::-1]]).reshape(layers, rank, width)
    left, right = products(phat, q)
    grp = ypos * cores + core
    own = lax.dynamic_slice_in_dim(left, grp * rows, rows, 2)
    spec = "lkr,lke->lre"
    approx = jnp.einsum(spec, own, right, preferred_element_type=F32) * (1.0 / reps)
    new_errors = merged - approx
    new_momenta = 0.9 * momenta + approx
    whole = jnp.einsum(spec, left, right, preferred_element_type=F32) * (1.0 / reps)
    new_weights = (old.astype(F32) - 0.5 * whole).astype(BF)

    bias_grad = bias * (scale / reps)
    new_bias_momenta = 0.9 * bias_momenta + lax.dynamic_slice_in_dim(bias_grad, grp * rows, rows, 1)
    new_biases = (old_b - 0.5 * bias_grad).astype(BF)
    return (new_weights, new_biases, new_errors[None], new_momenta, new_bias_momenta)


def solution(mesh):
    split = Mesh(mesh.devices.reshape(4, 4, 4, 2), ("x", "z", "y", "core"))
    rep, grp = ("x", "z"), ("y", "core")
    placed = (
        P(None, rep + grp, None),
        P(None, rep + grp, None),
        P(None, grp, None),
        P(None, grp),
        P(rep, None, grp, None),
        P(None, grp, None),
        P(None, grp),
        P(),
    )

    return jax.shard_map(
        body,
        mesh=split,
        in_specs=placed,
        out_specs=(P(), P(), P(rep, None, grp, None), P(None, grp, None), P(None, grp)),
        check_vma=False,
    )
```

```python
import jax
import jax.numpy as jnp
from jax import lax
from jax.experimental import pallas as pl
from jax.experimental.pallas import tpu as pltpu
from jax.sharding import Mesh
from jax.sharding import PartitionSpec as P


NS_STEPS = 5
HIGH = lax.Precision.HIGHEST
BF = jnp.bfloat16
F32 = jnp.float32


def ring(count, step):
    return [(i, (i + step) % count) for i in range(count)]


def pick(stack, index, axis=0):
    return lax.dynamic_index_in_dim(stack, index, axis, keepdims=False)


def hi_lo(row):
    high = row.astype(BF)
    low = (row - high.astype(F32)).astype(BF)
    return jnp.concatenate([high[None], low[None], jnp.zeros((6, row.shape[0]), BF)], 0)


def from_hi_lo(rows):
    return rows[0].astype(F32) + rows[1].astype(F32)


def paired(parts):
    return (parts[0] + parts[1]) + (parts[2] + parts[3])


def split3(value):
    one = value.astype(BF)
    rest = value - one.astype(F32)
    two = rest.astype(BF)
    three = (rest - two.astype(F32)).astype(BF)
    return jnp.concatenate([one, two, three], 0)


def by_three(left, right, dims):
    rank = left.shape[0]
    out = lax.dot_general(split3(left), right, dims, preferred_element_type=F32)
    return out[:rank] + out[rank : 2 * rank] + out[2 * rank :]


def exact(left, right, dims):
    return lax.dot_general(left, right, dims, precision=HIGH, preferred_element_type=F32)


NN = (((1,), (0,)), ((), ()))
NT = (((1,), (1,)), ((), ()))
TN = (((0,), (0,)), ((), ()))


def inverse_root(gram):
    fro = jnp.sqrt(jnp.sum(gram * gram, axis=(0, 1), keepdims=True)) + 1e-06
    rank = gram.shape[0]
    spot = lambda axis: lax.broadcasted_iota(jnp.int32, (rank, rank), axis)
    eye = jnp.where(spot(0) == spot(1), 1.0, 0.0).astype(F32)

    def step(pair):
        ymat, zmat = pair
        tmat = 1.5 * eye - 0.5 * exact(zmat, ymat, NN)
        return exact(ymat, tmat, NN), exact(tmat, zmat, NN)

    pair = (gram / fro, eye)
    for _ in range(NS_STEPS):
        pair = step(pair)
    zmat = pair[1]
    return zmat, jnp.sqrt(fro)


def half_round(q, rows_of_sum):
    p = by_three(q, rows_of_sum, NT)
    return p, exact(p, p, NT), by_three(p, rows_of_sum, NN)


def store_split(ref, at, value):
    rank, wide = value.shape
    high = value.astype(BF)
    ref[:rank, at : at + wide] = high
    ref[:rank, at + wide : at + 2 * wide] = (value - high.astype(F32)).astype(BF)


def widened(gram):
    rank = gram.shape[0]
    return jnp.concatenate([gram, jnp.zeros((rank, 128 - rank), F32)], 1)


def first_kernel(xpos_ref, *refs):
    parts, (q_ref, bias_ref, sum_ref, out_ref) = refs[:4], refs[4:]
    rank, width = q_ref.shape
    piece = parts[0].shape[0]
    xpos = xpos_ref[0]
    for j in range(4):
        value = parts[j][...]
        for spot in (1, 2, 3):
            value = jnp.where(xpos == spot, parts[spot ^ j][...], value)
        sum_ref[j * piece : (j + 1) * piece] = value
    rest = sum_ref.shape[0] - 4 * piece
    sum_ref[4 * piece :] = jnp.zeros((rest, width), BF)
    _, gram, u = half_round(q_ref[...], sum_ref[...])
    out_ref[:rank, :width] = u.astype(BF)
    store_split(out_ref, width, widened(gram))
    bias = bias_ref[...]
    high = bias.astype(BF).astype(F32)
    both = jnp.concatenate([high, bias - high, jnp.zeros((6, width), F32)], 0)
    both = jnp.concatenate([both, jnp.zeros((8, 256), F32)], 1)
    out_ref[rank:] = both.astype(BF)


def summed_parts(parts, columns):
    load = lambda ref: ref[:, :columns].astype(F32)
    return (load(parts[0]) + load(parts[1])) + (load(parts[2]) + load(parts[3]))


def second_kernel(*refs):
    parts, (far_ref, out_ref, bias_ref, sum_ref, arrived) = refs[:4], refs[4:]
    fetch = pltpu.make_async_copy(far_ref, sum_ref, arrived)
    fetch.start()
    width = sum_ref.shape[1]
    rank = out_ref.shape[0]
    total = summed_parts(parts, width + 256)
    gram = total[:rank, width : width + 128] + total[:rank, width + 128 :]
    zmat, root = inverse_root(gram[:, :rank])
    q = exact(zmat, total[:rank, :width], TN) / root
    bias = total[rank : rank + 1, :width] + total[rank + 1 : rank + 2, :width]
    bias_ref[...] = jnp.concatenate([bias, jnp.zeros((7, width), F32)], 0)
    fetch.wait()
    p, gram, u = half_round(q, sum_ref[...])
    out_ref[:, :width] = u.astype(BF)
    store_split(out_ref, width, widened(gram))
    store_split(out_ref, width + 256, p)


def third_kernel(*refs):
    parts, (q_ref, z_ref) = refs[:4], refs[4:]
    rank, width = q_ref.shape
    total = summed_parts(parts, width + 256)
    gram = total[:, width : width + 128] + total[:, width + 128 :]
    zmat, root = inverse_root(gram[:, :rank])
    q_ref[...] = exact(zmat, total[:, :width], TN) / root
    z_ref[...] = zmat / root


def lineup_kernel(ypos_ref, *refs):
    parts, out_ref = refs[:4], refs[4]
    for spot in range(4):

        @pl.when(ypos_ref[0] == spot)
        def _():
            def move(i, carry):
                at = pl.ds(pl.multiple_of(8 * i, 8), 8)
                for j in range(4):
                    for layer in range(out_ref.shape[1]):
                        out_ref[j, layer, at] = parts[spot ^ j][layer, at]
                return carry

            lax.fori_loop(0, out_ref.shape[2] // 8, move, 0)


def assemble_kernel(core_ref, mine_ref, theirs_ref, out_ref):
    rows = out_ref.shape[1] // 2
    for spot in range(2):

        @pl.when(core_ref[0] == spot)
        def _():
            for side in range(2):
                ref = mine_ref if side == spot else theirs_ref
                out_ref[:, side * rows : (side + 1) * rows] = ref[0, :, :rows]


def assemble(core, mine, theirs, rows):
    ys, layers, held, width = mine.shape
    block = pl.BlockSpec((1, layers, held, width), lambda j, core: (j, 0, 0, 0))
    return pl.pallas_call(
        assemble_kernel,
        out_shape=jax.ShapeDtypeStruct((layers, width, width), BF),
        grid_spec=pltpu.PrefetchScalarGridSpec(
            num_scalar_prefetch=1,
            grid=(ys,),
            in_specs=[block, block],
            out_specs=pl.BlockSpec((layers, 2 * rows, width), lambda j, core: (0, j, 0)),
        ),
        name="assemble",
    )(core, mine, theirs)


def in_vmem(kernel, outs, scalars=0, far=0, scratch=()):
    vmem = pl.BlockSpec(memory_space=pltpu.VMEM)
    smem = pl.BlockSpec(memory_space=pltpu.SMEM)

    def call(*args):
        return pl.pallas_call(
            kernel,
            out_shape=outs,
            in_specs=[smem] * scalars
            + [vmem] * (len(args) - scalars - far)
            + [pl.BlockSpec(memory_space=pl.ANY)] * far,
            scratch_shapes=list(scratch),
            out_specs=jax.tree.map(lambda _: vmem, outs),
            compiler_params=pltpu.CompilerParams(vmem_limit_bytes=24 << 20),
        )(*args)

    return call


def products(left, right):
    l1 = left.astype(BF)
    rest = left - l1.astype(F32)
    l2 = rest.astype(BF)
    l3 = (rest - l2.astype(F32)).astype(BF)
    r1 = right.astype(BF)
    rest = right - r1.astype(F32)
    r2 = rest.astype(BF)
    r3 = (rest - r2.astype(F32)).astype(BF)
    return (
        jnp.concatenate([l1, l1, l2, l1, l2, l3], -2),
        jnp.concatenate([r1, r2, r1, r3, r2, r1], -2),
    )


def body(inputs, out_grads, weights, biases, errors, momenta, bias_momenta, q_start):
    layers, tok, width = inputs.shape
    cores = lax.axis_size("core")
    ys = lax.axis_size("y")
    xs = lax.axis_size("x")
    reps = xs * lax.axis_size("z")
    rows = width // (cores * ys)
    rank = q_start.shape[-1]
    scale = float(tok) ** (-0.5)
    core, ypos, xpos = lax.axis_index("core"), lax.axis_index("y"), lax.axis_index("x")

    def swap(value):
        return lax.ppermute(value, "core", ring(cores, 1))

    def trade(value, axis, k):
        return lax.ppermute(value, axis, [(i, i ^ k) for i in range(4)])

    def everyone(value, axis):
        return [value] + [trade(value, axis, k) for k in (1, 2, 3)]

    def natural(parts, position):
        ordered = []
        for j in range(4):
            value = parts[j]
            for spot in (1, 2, 3):
                value = jnp.where(position == spot, parts[spot ^ j], value)
            ordered.append(value)
        return ordered

    old_m = lax.optimization_barrier(momenta)
    old = (weights.astype(F32) - 0.45 * old_m).astype(BF)
    row_b, row_m = lax.optimization_barrier((biases, bias_momenta))
    two = jnp.stack([row_b, row_m.astype(BF)], 1)
    old = jnp.concatenate([old, jnp.pad(two, ((0, 0), (0, 6), (0, width - rows)))], 1)
    parts = [old]
    for k in (1, 2, 3):
        parts.append(trade(old, "y", k))
    held = rows + 8
    mine = in_vmem(
        lineup_kernel, jax.ShapeDtypeStruct((ys, layers, held, width), BF), 1
    )(ypos.astype(jnp.int32)[None], *parts)
    theirs = swap(mine)
    old = assemble(core.astype(jnp.int32)[None], mine, theirs, rows)
    tails = [stack[:, :, rows : rows + 2, :rows].astype(F32) for stack in (mine, theirs)]
    tails = [tail[:, :, 0] - 0.45 * tail[:, :, 1] for tail in tails]
    even, odd = jnp.where(core == 0, *tails), jnp.where(core == 0, *tails[::-1])
    old_b = jnp.stack([even, odd], 1).transpose(2, 0, 1, 3).reshape(layers, width)

    def chip_blocks(layer, after=None):
        x, y = inputs, out_grads
        if after is not None:
            x, y, _ = lax.optimization_barrier((x, y, after))
        part = jnp.einsum("tr,te->re", x[layer], y[layer], preferred_element_type=F32).astype(BF)
        part = lax.optimization_barrier(part).reshape(ys * cores, rows, width)
        got = swap(
            pick(part.reshape(ys, cores, rows, width), 1 - core, 1)
        )
        blocks = []
        for k in range(4):
            there = ypos ^ k
            blocks.append(pick(part, there * cores + core).astype(F32) + pick(got, there).astype(F32))
        return blocks[0], [b.astype(BF) for b in blocks[1:]]

    def merge(layer, own, blocks):
        for k in (1, 2, 3):
            block = trade(blocks[k - 1], "y", k)
            own = own + block.astype(F32)
        return own * scale + errors[0, layer]

    own0, blocks0 = chip_blocks(0)
    own1, blocks1 = chip_blocks(1, blocks0)
    merged0 = lax.optimization_barrier(merge(0, own0, blocks0))
    merged = jnp.stack([merged0, merge(1, own1, blocks1)])
    col_sums = jnp.sum(out_grads, axis=1, dtype=F32)

    got = swap(
        jnp.concatenate([pick(merged, 1 - core).astype(BF), hi_lo(pick(col_sums, 1 - core))], 0)
    )
    own, got_rows = pick(merged, core), got[:rows].astype(F32)
    both = jnp.stack([jnp.where(core == 0, own, got_rows), jnp.where(core == 0, got_rows, own)])
    both = both.reshape(4, rows // 2, width)
    bias = pick(col_sums, core) + from_hi_lo(got[rows:])
    bias_rows = hi_lo(bias)
    half = rows // 2

    def loaded(main):
        return jnp.concatenate([main.astype(BF), bias_rows], 0)

    parts = []
    for k in (1, 2, 3):
        block = loaded(pick(both, xpos ^ k))
        parts.append(trade(block, "x", k))
    main = paired([pick(both, xpos)] + [p[:half].astype(F32) for p in parts])
    bias = paired([from_hi_lo(p) for p in [bias_rows] + [p[half:] for p in parts]])
    bias_rows = hi_lo(bias)
    parts = everyone(loaded(main), "z")
    main = paired([p[:half].astype(F32) for p in parts]).astype(BF)
    bias = paired([from_hi_lo(p[half:]) for p in parts])
    parts = everyone(main, "x")
    shape = lambda *dims, of: jax.ShapeDtypeStruct(dims, of)
    q = pick(q_start, core).T
    total, packed = in_vmem(
        first_kernel, (shape(384, width, of=BF), shape(rank + 8, width + 256, of=BF)), 1
    )(xpos.astype(jnp.int32)[None], *parts, q, bias[None])
    parts = everyone(packed, "y")
    packed, bias_rows = in_vmem(
        second_kernel,
        (shape(rank, width + 1024, of=BF), shape(8, width, of=F32)),
        far=1,
        scratch=(pltpu.VMEM((384, width), BF), pltpu.SemaphoreType.DMA),
    )(*parts, total)
    parts = everyone(packed, "y")
    other = swap(bias_rows)
    bias = jnp.stack([jnp.where(core == l, bias_rows[0], other[0]) for l in range(layers)])
    bias_grad = bias * (scale / reps)
    grp = ypos * cores + core
    bias_own = lax.dynamic_slice_in_dim(bias_grad, grp * rows, rows, 1)
    new_bias_momenta = 0.9 * bias_momenta + bias_own
    new_biases = (old_b - 0.5 * bias_grad).astype(BF)
    q, zmat = in_vmem(third_kernel, (shape(rank, width, of=F32), shape(rank, rank, of=F32)))(*parts)
    at = width + 256
    p_all = [
        part[:, at : at + 2 * rows].astype(F32) + part[:, at + 384 : at + 384 + 2 * rows].astype(F32)
        for part in parts
    ]
    p_all = jnp.concatenate(natural(p_all, ypos), 1)
    phat = exact(zmat, p_all, TN)

    packed = jnp.concatenate([q, phat], 1)
    other = swap(packed)
    pair = [jnp.where(core == layer, packed, other) for layer in range(layers)]
    q = jnp.stack([p[:, :width] for p in pair])
    phat = jnp.stack([p[:, width:] for p in pair])
    left, right = products(phat, q)
    own = lax.dynamic_slice_in_dim(left, grp * rows, rows, 2)
    spec = "lkr,lke->lre"
    approx = jnp.einsum(spec, own, right, preferred_element_type=F32) * (1.0 / reps)
    new_errors = merged - approx
    new_momenta = 0.9 * momenta + approx
    whole = jnp.einsum(spec, left, right, preferred_element_type=F32) * (1.0 / reps)
    new_weights = (old.astype(F32) - 0.5 * whole).astype(BF)

    return (new_weights, new_biases, new_errors[None], new_momenta, new_bias_momenta)


def solution(mesh):
    split = Mesh(mesh.devices.reshape(4, 4, 4, 2), ("x", "z", "y", "core"))
    rep, grp = ("x", "z"), ("y", "core")
    placed = (
        P(None, rep + grp, None),
        P(None, rep + grp, None),
        P(None, grp, None),
        P(None, grp),
        P(rep, None, grp, None),
        P(None, grp, None),
        P(None, grp),
        P(),
    )

    return jax.shard_map(
        body,
        mesh=split,
        in_specs=placed,
        out_specs=(P(), P(), P(rep, None, grp, None), P(None, grp, None), P(None, grp)),
        check_vma=False,
    )
```

```python
import jax
import jax.numpy as jnp
from jax import lax
from jax.experimental import pallas as pl
from jax.experimental.pallas import tpu as pltpu
from jax.sharding import Mesh
from jax.sharding import PartitionSpec as P


NS_STEPS = 5
HIGH = lax.Precision.HIGHEST
BF = jnp.bfloat16
F32 = jnp.float32


def ring(count, step):
    return [(i, (i + step) % count) for i in range(count)]


def pick(stack, index, axis=0):
    return lax.dynamic_index_in_dim(stack, index, axis, keepdims=False)


def hi_lo(row):
    high = row.astype(BF)
    low = (row - high.astype(F32)).astype(BF)
    return jnp.concatenate([high[None], low[None], jnp.zeros((6, row.shape[0]), BF)], 0)


def from_hi_lo(rows):
    return rows[0].astype(F32) + rows[1].astype(F32)


def paired(parts):
    return (parts[0] + parts[1]) + (parts[2] + parts[3])


def split3(value):
    one = value.astype(BF)
    rest = value - one.astype(F32)
    two = rest.astype(BF)
    three = (rest - two.astype(F32)).astype(BF)
    return jnp.concatenate([one, two, three], 0)


def by_three(left, right, dims):
    rank = left.shape[0]
    out = lax.dot_general(split3(left), right, dims, preferred_element_type=F32)
    return out[:rank] + out[rank : 2 * rank] + out[2 * rank :]


def exact(left, right, dims):
    return lax.dot_general(left, right, dims, precision=HIGH, preferred_element_type=F32)


NN = (((1,), (0,)), ((), ()))
NT = (((1,), (1,)), ((), ()))
TN = (((0,), (0,)), ((), ()))


def inverse_root(gram):
    fro = jnp.sqrt(jnp.sum(gram * gram, axis=(0, 1), keepdims=True)) + 1e-06
    rank = gram.shape[0]
    spot = lambda axis: lax.broadcasted_iota(jnp.int32, (rank, rank), axis)
    eye = jnp.where(spot(0) == spot(1), 1.0, 0.0).astype(F32)

    def step(pair):
        ymat, zmat = pair
        tmat = 1.5 * eye - 0.5 * exact(zmat, ymat, NN)
        return exact(ymat, tmat, NN), exact(tmat, zmat, NN)

    pair = (gram / fro, eye)
    for _ in range(NS_STEPS):
        pair = step(pair)
    zmat = pair[1]
    return zmat, jnp.sqrt(fro)


def half_round(q, rows_of_sum):
    p = by_three(q, rows_of_sum, NT)
    return p, exact(p, p, NT), by_three(p, rows_of_sum, NN)


def store_split(ref, at, value):
    rank, wide = value.shape
    high = value.astype(BF)
    ref[:rank, at : at + wide] = high
    ref[:rank, at + wide : at + 2 * wide] = (value - high.astype(F32)).astype(BF)


def widened(gram):
    rank = gram.shape[0]
    return jnp.concatenate([gram, jnp.zeros((rank, 128 - rank), F32)], 1)


def first_kernel(xpos_ref, *refs):
    parts, (q_ref, bias_ref, sum_ref, out_ref) = refs[:4], refs[4:]
    rank, width = q_ref.shape
    piece = parts[0].shape[0]
    xpos = xpos_ref[0]
    for j in range(4):
        value = parts[j][...]
        for spot in (1, 2, 3):
            value = jnp.where(xpos == spot, parts[spot ^ j][...], value)
        sum_ref[j * piece : (j + 1) * piece] = value
    rest = sum_ref.shape[0] - 4 * piece
    sum_ref[4 * piece :] = jnp.zeros((rest, width), BF)
    _, gram, u = half_round(q_ref[...], sum_ref[...])
    out_ref[:rank, :width] = u.astype(BF)
    store_split(out_ref, width, widened(gram))
    bias = bias_ref[...]
    high = bias.astype(BF).astype(F32)
    both = jnp.concatenate([high, bias - high, jnp.zeros((6, width), F32)], 0)
    both = jnp.concatenate([both, jnp.zeros((8, 256), F32)], 1)
    out_ref[rank:] = both.astype(BF)


def summed_parts(parts, columns):
    load = lambda ref: ref[:, :columns].astype(F32)
    return (load(parts[0]) + load(parts[1])) + (load(parts[2]) + load(parts[3]))


def second_kernel(*refs):
    parts, (far_ref, out_ref, bias_ref, sum_ref, arrived) = refs[:4], refs[4:]
    fetch = pltpu.make_async_copy(far_ref, sum_ref, arrived)
    fetch.start()
    width = sum_ref.shape[1]
    rank = out_ref.shape[0]
    total = summed_parts(parts, width + 256)
    gram = total[:rank, width : width + 128] + total[:rank, width + 128 :]
    zmat, root = inverse_root(gram[:, :rank])
    q = exact(zmat, total[:rank, :width], TN) / root
    bias = total[rank : rank + 1, :width] + total[rank + 1 : rank + 2, :width]
    bias_ref[...] = jnp.concatenate([bias, jnp.zeros((7, width), F32)], 0)
    fetch.wait()
    p, gram, u = half_round(q, sum_ref[...])
    out_ref[:, :width] = u.astype(BF)
    store_split(out_ref, width, widened(gram))
    store_split(out_ref, width + 256, p)


def third_kernel(*refs):
    parts, (q_ref, z_ref) = refs[:4], refs[4:]
    rank, width = q_ref.shape
    total = summed_parts(parts, width + 256)
    gram = total[:, width : width + 128] + total[:, width + 128 :]
    zmat, root = inverse_root(gram[:, :rank])
    q_ref[...] = exact(zmat, total[:, :width], TN) / root
    z_ref[...] = zmat / root


def lineup_kernel(ypos_ref, *refs):
    parts, out_ref = refs[:4], refs[4]
    for spot in range(4):

        @pl.when(ypos_ref[0] == spot)
        def _():
            for j in range(4):
                out_ref[j] = parts[spot ^ j][...]


def lineup(ypos, parts):
    layers, held, width = parts[0].shape
    block = pl.BlockSpec((1, held, width), lambda i, ypos: (i, 0, 0))
    return pl.pallas_call(
        lineup_kernel,
        out_shape=jax.ShapeDtypeStruct((4, layers, held, width), BF),
        grid_spec=pltpu.PrefetchScalarGridSpec(
            num_scalar_prefetch=1,
            grid=(layers,),
            in_specs=[block] * 4,
            out_specs=pl.BlockSpec((4, 1, held, width), lambda i, ypos: (0, i, 0, 0)),
        ),
        name="lineup",
    )(ypos, *parts)


def assemble_kernel(core_ref, mine_ref, theirs_ref, out_ref):
    rows = out_ref.shape[1] // 2
    for spot in range(2):

        @pl.when(core_ref[0] == spot)
        def _():
            for side in range(2):
                ref = mine_ref if side == spot else theirs_ref
                out_ref[:, side * rows : (side + 1) * rows] = ref[0, :, :rows]


def assemble(core, mine, theirs, rows):
    ys, layers, held, width = mine.shape
    block = pl.BlockSpec((1, layers, held, width), lambda j, core: (j, 0, 0, 0))
    return pl.pallas_call(
        assemble_kernel,
        out_shape=jax.ShapeDtypeStruct((layers, width, width), BF),
        grid_spec=pltpu.PrefetchScalarGridSpec(
            num_scalar_prefetch=1,
            grid=(ys,),
            in_specs=[block, block],
            out_specs=pl.BlockSpec((layers, 2 * rows, width), lambda j, core: (0, j, 0)),
        ),
        name="assemble",
    )(core, mine, theirs)


def in_vmem(kernel, outs, scalars=0, far=0, scratch=()):
    vmem = pl.BlockSpec(memory_space=pltpu.VMEM)
    smem = pl.BlockSpec(memory_space=pltpu.SMEM)

    def call(*args):
        return pl.pallas_call(
            kernel,
            out_shape=outs,
            in_specs=[smem] * scalars
            + [vmem] * (len(args) - scalars - far)
            + [pl.BlockSpec(memory_space=pl.ANY)] * far,
            scratch_shapes=list(scratch),
            out_specs=jax.tree.map(lambda _: vmem, outs),
            compiler_params=pltpu.CompilerParams(vmem_limit_bytes=24 << 20),
        )(*args)

    return call


def products(left, right):
    l1 = left.astype(BF)
    rest = left - l1.astype(F32)
    l2 = rest.astype(BF)
    l3 = (rest - l2.astype(F32)).astype(BF)
    r1 = right.astype(BF)
    rest = right - r1.astype(F32)
    r2 = rest.astype(BF)
    r3 = (rest - r2.astype(F32)).astype(BF)
    return (
        jnp.concatenate([l1, l1, l2, l1, l2, l3], -2),
        jnp.concatenate([r1, r2, r1, r3, r2, r1], -2),
    )


def body(inputs, out_grads, weights, biases, errors, momenta, bias_momenta, q_start):
    layers, tok, width = inputs.shape
    cores = lax.axis_size("core")
    ys = lax.axis_size("y")
    xs = lax.axis_size("x")
    reps = xs * lax.axis_size("z")
    rows = width // (cores * ys)
    rank = q_start.shape[-1]
    scale = float(tok) ** (-0.5)
    core, ypos, xpos = lax.axis_index("core"), lax.axis_index("y"), lax.axis_index("x")

    def swap(value):
        return lax.ppermute(value, "core", ring(cores, 1))

    def trade(value, axis, k):
        return lax.ppermute(value, axis, [(i, i ^ k) for i in range(4)])

    def everyone(value, axis):
        return [value] + [trade(value, axis, k) for k in (1, 2, 3)]

    def natural(parts, position):
        ordered = []
        for j in range(4):
            value = parts[j]
            for spot in (1, 2, 3):
                value = jnp.where(position == spot, parts[spot ^ j], value)
            ordered.append(value)
        return ordered

    old_m = lax.optimization_barrier(momenta)
    old = (weights.astype(F32) - 0.45 * old_m).astype(BF)
    row_b, row_m = lax.optimization_barrier((biases, bias_momenta))
    two = jnp.stack([row_b, row_m.astype(BF)], 1)
    old = jnp.concatenate([old, jnp.pad(two, ((0, 0), (0, 6), (0, width - rows)))], 1)
    parts = [old]
    for k in (1, 2, 3):
        parts.append(trade(old, "y", k))
    mine = lineup(ypos.astype(jnp.int32)[None], parts)
    theirs = swap(mine)
    old = assemble(core.astype(jnp.int32)[None], mine, theirs, rows)
    tails = [stack[:, :, rows : rows + 2, :rows].astype(F32) for stack in (mine, theirs)]
    tails = [tail[:, :, 0] - 0.45 * tail[:, :, 1] for tail in tails]
    even, odd = jnp.where(core == 0, *tails), jnp.where(core == 0, *tails[::-1])
    old_b = jnp.stack([even, odd], 1).transpose(2, 0, 1, 3).reshape(layers, width)

    def chip_blocks(layer, after=None):
        x, y = inputs, out_grads
        if after is not None:
            x, y, _ = lax.optimization_barrier((x, y, after))
        part = jnp.einsum("tr,te->re", x[layer], y[layer], preferred_element_type=F32).astype(BF)
        part = lax.optimization_barrier(part).reshape(ys * cores, rows, width)
        got = swap(
            pick(part.reshape(ys, cores, rows, width), 1 - core, 1)
        )
        blocks = []
        for k in range(4):
            there = ypos ^ k
            blocks.append(pick(part, there * cores + core).astype(F32) + pick(got, there).astype(F32))
        return blocks[0], [b.astype(BF) for b in blocks[1:]]

    def merge(layer, own, blocks):
        for k in (1, 2, 3):
            block = trade(blocks[k - 1], "y", k)
            own = own + block.astype(F32)
        held = errors if layer else lax.optimization_barrier(errors)
        return own * scale + held[0, layer]

    own0, blocks0 = chip_blocks(0)
    own1, blocks1 = chip_blocks(1, blocks0)
    merged0 = lax.optimization_barrier(merge(0, own0, blocks0))
    merged = jnp.stack([merged0, merge(1, own1, blocks1)])
    col_sums = jnp.sum(out_grads, axis=1, dtype=F32)

    got = swap(
        jnp.concatenate([pick(merged, 1 - core).astype(BF), hi_lo(pick(col_sums, 1 - core))], 0)
    )
    own, got_rows = pick(merged, core), got[:rows].astype(F32)
    both = jnp.stack([jnp.where(core == 0, own, got_rows), jnp.where(core == 0, got_rows, own)])
    both = both.reshape(4, rows // 2, width)
    bias = pick(col_sums, core) + from_hi_lo(got[rows:])
    bias_rows = hi_lo(bias)
    half = rows // 2

    def loaded(main):
        return jnp.concatenate([main.astype(BF), bias_rows], 0)

    parts = []
    for k in (1, 2, 3):
        block = loaded(pick(both, xpos ^ k))
        parts.append(trade(block, "x", k))
    main = paired([pick(both, xpos)] + [p[:half].astype(F32) for p in parts])
    bias = paired([from_hi_lo(p) for p in [bias_rows] + [p[half:] for p in parts]])
    bias_rows = hi_lo(bias)
    parts = everyone(loaded(main), "z")
    main = paired([p[:half].astype(F32) for p in parts]).astype(BF)
    bias = paired([from_hi_lo(p[half:]) for p in parts])
    parts = everyone(main, "x")
    shape = lambda *dims, of: jax.ShapeDtypeStruct(dims, of)
    q = pick(q_start, core).T
    total, packed = in_vmem(
        first_kernel, (shape(384, width, of=BF), shape(rank + 8, width + 256, of=BF)), 1
    )(xpos.astype(jnp.int32)[None], *parts, q, bias[None])
    parts = everyone(packed, "y")
    packed, bias_rows = in_vmem(
        second_kernel,
        (shape(rank, width + 1024, of=BF), shape(8, width, of=F32)),
        far=1,
        scratch=(pltpu.VMEM((384, width), BF), pltpu.SemaphoreType.DMA),
    )(*parts, total)
    parts = everyone(packed, "y")
    other = swap(bias_rows)
    bias = jnp.stack([jnp.where(core == l, bias_rows[0], other[0]) for l in range(layers)])
    bias_grad = bias * (scale / reps)
    grp = ypos * cores + core
    bias_own = lax.dynamic_slice_in_dim(bias_grad, grp * rows, rows, 1)
    new_bias_momenta = 0.9 * bias_momenta + bias_own
    new_biases = (old_b - 0.5 * bias_grad).astype(BF)
    q, zmat = in_vmem(third_kernel, (shape(rank, width, of=F32), shape(rank, rank, of=F32)))(*parts)
    at = width + 256
    p_all = [
        part[:, at : at + 2 * rows].astype(F32) + part[:, at + 384 : at + 384 + 2 * rows].astype(F32)
        for part in parts
    ]
    p_all = jnp.concatenate(natural(p_all, ypos), 1)
    phat = exact(zmat, p_all, TN)

    packed = jnp.concatenate([q, phat], 1)
    other = swap(packed)
    pair = [jnp.where(core == layer, packed, other) for layer in range(layers)]
    q = jnp.stack([p[:, :width] for p in pair])
    phat = jnp.stack([p[:, width:] for p in pair])
    left, right = products(phat, q)
    own = lax.dynamic_slice_in_dim(left, grp * rows, rows, 2)
    spec = "lkr,lke->lre"
    approx = jnp.einsum(spec, own, right, preferred_element_type=F32) * (1.0 / reps)
    new_errors = merged - approx
    new_momenta = 0.9 * momenta + approx
    whole = jnp.einsum(spec, left, right, preferred_element_type=F32) * (1.0 / reps)
    new_weights = (old.astype(F32) - 0.5 * whole).astype(BF)

    return (new_weights, new_biases, new_errors[None], new_momenta, new_bias_momenta)


def solution(mesh):
    split = Mesh(mesh.devices.reshape(4, 4, 4, 2), ("x", "z", "y", "core"))
    rep, grp = ("x", "z"), ("y", "core")
    placed = (
        P(None, rep + grp, None),
        P(None, rep + grp, None),
        P(None, grp, None),
        P(None, grp),
        P(rep, None, grp, None),
        P(None, grp, None),
        P(None, grp),
        P(),
    )

    return jax.shard_map(
        body,
        mesh=split,
        in_specs=placed,
        out_specs=(P(), P(), P(rep, None, grp, None), P(None, grp, None), P(None, grp)),
        check_vma=False,
    )
```

```python
import jax
import jax.numpy as jnp
from jax import lax
from jax.experimental import pallas as pl
from jax.experimental.pallas import tpu as pltpu
from jax.sharding import Mesh
from jax.sharding import PartitionSpec as P


NS_STEPS = 5
HIGH = lax.Precision.HIGHEST
BF = jnp.bfloat16
F32 = jnp.float32


def ring(count, step):
    return [(i, (i + step) % count) for i in range(count)]


def pick(stack, index, axis=0):
    return lax.dynamic_index_in_dim(stack, index, axis, keepdims=False)


def hi_lo(row):
    high = row.astype(BF)
    low = (row - high.astype(F32)).astype(BF)
    return jnp.concatenate([high[None], low[None], jnp.zeros((6, row.shape[0]), BF)], 0)


def from_hi_lo(rows):
    return rows[0].astype(F32) + rows[1].astype(F32)


def paired(parts):
    return (parts[0] + parts[2]) + (parts[1] + parts[3])


def split3(value):
    one = value.astype(BF)
    rest = value - one.astype(F32)
    two = rest.astype(BF)
    three = (rest - two.astype(F32)).astype(BF)
    return jnp.concatenate([one, two, three], 0)


def by_three(left, right, dims):
    rank = left.shape[0]
    out = lax.dot_general(split3(left), right, dims, preferred_element_type=F32)
    return out[:rank] + out[rank : 2 * rank] + out[2 * rank :]


def exact(left, right, dims):
    return lax.dot_general(left, right, dims, precision=HIGH, preferred_element_type=F32)


NN = (((1,), (0,)), ((), ()))
NT = (((1,), (1,)), ((), ()))
TN = (((0,), (0,)), ((), ()))


def inverse_root(gram):
    fro = jnp.sqrt(jnp.sum(gram * gram, axis=(0, 1), keepdims=True)) + 1e-06
    rank = gram.shape[0]
    spot = lambda axis: lax.broadcasted_iota(jnp.int32, (rank, rank), axis)
    eye = jnp.where(spot(0) == spot(1), 1.0, 0.0).astype(F32)

    def step(pair):
        ymat, zmat = pair
        tmat = 1.5 * eye - 0.5 * exact(zmat, ymat, NN)
        return exact(ymat, tmat, NN), exact(tmat, zmat, NN)

    pair = (gram / fro, eye)
    for _ in range(NS_STEPS):
        pair = step(pair)
    zmat = pair[1]
    return zmat, jnp.sqrt(fro)


def half_round(q, rows_of_sum):
    p = by_three(q, rows_of_sum, NT)
    return p, exact(p, p, NT), by_three(p, rows_of_sum, NN)


def store_split(ref, at, value):
    rank, wide = value.shape
    high = value.astype(BF)
    ref[:rank, at : at + wide] = high
    ref[:rank, at + wide : at + 2 * wide] = (value - high.astype(F32)).astype(BF)


def widened(gram):
    rank = gram.shape[0]
    return jnp.concatenate([gram, jnp.zeros((rank, 128 - rank), F32)], 1)


def first_kernel(xpos_ref, *refs):
    parts, (q_ref, bias_ref, sum_ref, out_ref) = refs[:4], refs[4:]
    rank, width = q_ref.shape
    piece = parts[0].shape[0]
    xpos = xpos_ref[0]
    for j in range(4):
        value = parts[j][...]
        for spot in (1, 2, 3):
            value = jnp.where(xpos == spot, parts[spot ^ j][...], value)
        sum_ref[j * piece : (j + 1) * piece] = value
    rest = sum_ref.shape[0] - 4 * piece
    sum_ref[4 * piece :] = jnp.zeros((rest, width), BF)
    _, gram, u = half_round(q_ref[...], sum_ref[...])
    out_ref[:rank, :width] = u.astype(BF)
    store_split(out_ref, width, widened(gram))
    bias = bias_ref[...]
    high = bias.astype(BF).astype(F32)
    both = jnp.concatenate([high, bias - high, jnp.zeros((6, width), F32)], 0)
    both = jnp.concatenate([both, jnp.zeros((8, 256), F32)], 1)
    out_ref[rank:] = both.astype(BF)


def summed_parts(parts, columns):
    load = lambda ref: ref[:, :columns].astype(F32)
    return (load(parts[0]) + load(parts[1])) + (load(parts[2]) + load(parts[3]))


def second_kernel(*refs):
    parts, (far_ref, out_ref, bias_ref, sum_ref, arrived) = refs[:4], refs[4:]
    fetch = pltpu.make_async_copy(far_ref, sum_ref, arrived)
    fetch.start()
    width = sum_ref.shape[1]
    rank = out_ref.shape[0]
    total = summed_parts(parts, width + 256)
    gram = total[:rank, width : width + 128] + total[:rank, width + 128 :]
    zmat, root = inverse_root(gram[:, :rank])
    q = exact(zmat, total[:rank, :width], TN) / root
    bias = total[rank : rank + 1, :width] + total[rank + 1 : rank + 2, :width]
    bias_ref[...] = jnp.concatenate([bias, jnp.zeros((7, width), F32)], 0)
    fetch.wait()
    p, gram, u = half_round(q, sum_ref[...])
    out_ref[:, :width] = u.astype(BF)
    store_split(out_ref, width, widened(gram))
    store_split(out_ref, width + 256, p)


def third_kernel(*refs):
    parts, (q_ref, z_ref) = refs[:4], refs[4:]
    rank, width = q_ref.shape
    total = summed_parts(parts, width + 256)
    gram = total[:, width : width + 128] + total[:, width + 128 :]
    zmat, root = inverse_root(gram[:, :rank])
    q_ref[...] = exact(zmat, total[:, :width], TN) / root
    z_ref[...] = zmat / root


def lineup_kernel(ypos_ref, *refs):
    parts, out_ref = refs[:4], refs[4]
    for spot in range(4):

        @pl.when(ypos_ref[0] == spot)
        def _():
            for j in range(4):
                out_ref[j] = parts[spot ^ j][...]


def lineup(ypos, parts):
    layers, held, width = parts[0].shape
    block = pl.BlockSpec((1, held, width), lambda i, ypos: (i, 0, 0))
    return pl.pallas_call(
        lineup_kernel,
        out_shape=jax.ShapeDtypeStruct((4, layers, held, width), BF),
        grid_spec=pltpu.PrefetchScalarGridSpec(
            num_scalar_prefetch=1,
            grid=(layers,),
            in_specs=[block] * 4,
            out_specs=pl.BlockSpec((4, 1, held, width), lambda i, ypos: (0, i, 0, 0)),
        ),
        name="lineup",
    )(ypos, *parts)


def assemble_kernel(core_ref, mine_ref, theirs_ref, out_ref):
    rows = out_ref.shape[1] // 2
    for spot in range(2):

        @pl.when(core_ref[0] == spot)
        def _():
            for side in range(2):
                ref = mine_ref if side == spot else theirs_ref
                out_ref[:, side * rows : (side + 1) * rows] = ref[0, :, :rows]


def assemble(core, mine, theirs, rows):
    ys, layers, held, width = mine.shape
    block = pl.BlockSpec((1, layers, held, width), lambda j, core: (j, 0, 0, 0))
    return pl.pallas_call(
        assemble_kernel,
        out_shape=jax.ShapeDtypeStruct((layers, width, width), BF),
        grid_spec=pltpu.PrefetchScalarGridSpec(
            num_scalar_prefetch=1,
            grid=(ys,),
            in_specs=[block, block],
            out_specs=pl.BlockSpec((layers, 2 * rows, width), lambda j, core: (0, j, 0)),
        ),
        name="assemble",
    )(core, mine, theirs)


def in_vmem(kernel, outs, scalars=0, far=0, scratch=()):
    vmem = pl.BlockSpec(memory_space=pltpu.VMEM)
    smem = pl.BlockSpec(memory_space=pltpu.SMEM)

    def call(*args):
        return pl.pallas_call(
            kernel,
            out_shape=outs,
            in_specs=[smem] * scalars
            + [vmem] * (len(args) - scalars - far)
            + [pl.BlockSpec(memory_space=pl.ANY)] * far,
            scratch_shapes=list(scratch),
            out_specs=jax.tree.map(lambda _: vmem, outs),
            compiler_params=pltpu.CompilerParams(vmem_limit_bytes=24 << 20),
        )(*args)

    return call


def products(left, right):
    l1 = left.astype(BF)
    rest = left - l1.astype(F32)
    l2 = rest.astype(BF)
    l3 = (rest - l2.astype(F32)).astype(BF)
    r1 = right.astype(BF)
    rest = right - r1.astype(F32)
    r2 = rest.astype(BF)
    r3 = (rest - r2.astype(F32)).astype(BF)
    return (
        jnp.concatenate([l1, l1, l2, l1, l2, l3], -2),
        jnp.concatenate([r1, r2, r1, r3, r2, r1], -2),
    )


def body(inputs, out_grads, weights, biases, errors, momenta, bias_momenta, q_start):
    layers, tok, width = inputs.shape
    cores = lax.axis_size("core")
    ys = lax.axis_size("y")
    xs = lax.axis_size("x")
    reps = xs * lax.axis_size("z")
    rows = width // (cores * ys)
    rank = q_start.shape[-1]
    scale = float(tok) ** (-0.5)
    core, ypos, xpos = lax.axis_index("core"), lax.axis_index("y"), lax.axis_index("x")

    def swap(value):
        return lax.ppermute(value, "core", ring(cores, 1))

    def trade(value, axis, k):
        return lax.ppermute(value, axis, [(i, i ^ k) for i in range(4)])

    def from_back(value, axis, k):
        return lax.ppermute(value, axis, ring(4, k))

    def everyone(value, axis):
        return [value] + [trade(value, axis, k) for k in (1, 2, 3)]

    def natural(parts, position):
        ordered = []
        for j in range(4):
            value = parts[j]
            for spot in (1, 2, 3):
                value = jnp.where(position == spot, parts[spot ^ j], value)
            ordered.append(value)
        return ordered

    old_m = lax.optimization_barrier(momenta)
    old = (weights.astype(F32) - 0.45 * old_m).astype(BF)
    row_b, row_m = lax.optimization_barrier((biases, bias_momenta))
    two = jnp.stack([row_b, row_m.astype(BF)], 1)
    old = jnp.concatenate([old, jnp.pad(two, ((0, 0), (0, 6), (0, width - rows)))], 1)
    parts = [old]
    for k in (1, 2, 3):
        parts.append(trade(old, "y", k))
    mine = lineup(ypos.astype(jnp.int32)[None], parts)
    theirs = swap(mine)
    old = assemble(core.astype(jnp.int32)[None], mine, theirs, rows)
    tail = mine[:, :, rows : rows + 2, :rows].astype(F32)
    tail = tail[:, :, 0] - 0.45 * tail[:, :, 1]
    even, odd = jnp.where(core == 0, tail, 0.0), jnp.where(core == 0, 0.0, tail)
    pieces = [side[j] for j in range(ys) for side in (even, odd)]
    half_b = jnp.concatenate(pieces, -1)

    def chip_blocks(layer, after=None):
        x, y = inputs, out_grads
        if after is not None:
            x, y, _ = lax.optimization_barrier((x, y, after))
        part = jnp.einsum("tr,te->re", x[layer], y[layer], preferred_element_type=F32).astype(BF)
        part = lax.optimization_barrier(part).reshape(ys * cores, rows, width)
        got = swap(
            pick(part.reshape(ys, cores, rows, width), 1 - core, 1)
        )
        keep = lax.optimization_barrier(pick(part.reshape(ys, cores, rows, width), core, 1))
        blocks = []
        for k in range(4):
            there = ypos ^ k
            blocks.append(pick(keep, there).astype(F32) + pick(got, there).astype(F32))
        return blocks[0], [b.astype(BF) for b in blocks[1:]]

    def merge(layer, own, blocks):
        for k in (1, 2, 3):
            block = trade(blocks[k - 1], "y", k)
            own = own + block.astype(F32)
        held = errors if layer else lax.optimization_barrier(errors)
        return own * scale + held[0, layer]

    own0, blocks0 = chip_blocks(0)
    own1, blocks1 = chip_blocks(1, blocks0)
    merged0 = lax.optimization_barrier(merge(0, own0, blocks0))
    merged = jnp.stack([merged0, merge(1, own1, blocks1)])
    col_sums = jnp.sum(out_grads, axis=1, dtype=F32)

    got = swap(
        jnp.concatenate([pick(merged, 1 - core).astype(BF), hi_lo(pick(col_sums, 1 - core))], 0)
    )
    own, got_rows = pick(merged, core), got[:rows].astype(F32)
    both = jnp.stack([jnp.where(core == 0, own, got_rows), jnp.where(core == 0, got_rows, own)])
    both = both.reshape(4, rows // 2, width)
    bias = pick(col_sums, core) + from_hi_lo(got[rows:])
    bias_rows = hi_lo(bias)
    half = rows // 2

    def loaded(main):
        return jnp.concatenate([main.astype(BF), bias_rows], 0)

    parts = []
    for k in (1, 2, 3):
        block = loaded(pick(both, (xpos + k) % 4))
        parts.append(from_back(block, "x", k))
    main = paired([pick(both, xpos)] + [p[:half].astype(F32) for p in parts])
    bias = paired([from_hi_lo(p) for p in [bias_rows] + [p[half:] for p in parts]])
    bias_rows = hi_lo(bias)
    block = loaded(main)
    parts = [block] + [from_back(block, "z", k) for k in (1, 2, 3)]
    main = paired([p[:half].astype(F32) for p in parts]).astype(BF)
    bias = paired([from_hi_lo(p[half:]) for p in parts])
    parts = everyone(main, "x")
    shape = lambda *dims, of: jax.ShapeDtypeStruct(dims, of)
    q = pick(q_start, core).T
    total, packed = in_vmem(
        first_kernel, (shape(384, width, of=BF), shape(rank + 8, width + 256, of=BF)), 1
    )(xpos.astype(jnp.int32)[None], *parts, q, bias[None])
    parts = everyone(packed, "y")
    packed, bias_rows = in_vmem(
        second_kernel,
        (shape(rank, width + 1024, of=BF), shape(8, width, of=F32)),
        far=1,
        scratch=(pltpu.VMEM((384, width), BF), pltpu.SemaphoreType.DMA),
    )(*parts, total)
    parts = everyone(packed, "y")
    bias_rows = jnp.concatenate([bias_rows[:1], half_b, bias_rows[3:]], 0)
    other = swap(bias_rows)
    bias = jnp.stack([jnp.where(core == l, bias_rows[0], other[0]) for l in range(layers)])
    bias_grad = bias * (scale / reps)
    grp = ypos * cores + core
    bias_own = lax.dynamic_slice_in_dim(bias_grad, grp * rows, rows, 1)
    new_bias_momenta = 0.9 * bias_momenta + bias_own
    old_b = bias_rows[1:3] + other[1:3]
    new_biases = (old_b - 0.5 * bias_grad).astype(BF)
    q, zmat = in_vmem(third_kernel, (shape(rank, width, of=F32), shape(rank, rank, of=F32)))(*parts)
    at = width + 256
    p_all = [
        part[:, at : at + 2 * rows].astype(F32) + part[:, at + 384 : at + 384 + 2 * rows].astype(F32)
        for part in parts
    ]
    p_all = jnp.concatenate(natural(p_all, ypos), 1)
    phat = exact(zmat, p_all, TN)

    packed = jnp.concatenate([q, phat], 1)
    other = swap(packed)
    pair = [jnp.where(core == layer, packed, other) for layer in range(layers)]
    q = jnp.stack([p[:, :width] for p in pair])
    phat = jnp.stack([p[:, width:] for p in pair])
    left, right = products(phat, q)
    own = lax.dynamic_slice_in_dim(left, grp * rows, rows, 2)
    spec = "lkr,lke->lre"
    approx = jnp.einsum(spec, own, right, preferred_element_type=F32) * (1.0 / reps)
    new_errors = merged - approx
    new_momenta = 0.9 * momenta + approx
    whole = jnp.einsum(spec, left, right, preferred_element_type=F32) * (1.0 / reps)
    new_weights = (old.astype(F32) - 0.5 * whole).astype(BF)

    return (new_weights, new_biases, new_errors[None], new_momenta, new_bias_momenta)


def solution(mesh):
    split = Mesh(mesh.devices.reshape(4, 4, 4, 2), ("x", "z", "y", "core"))
    rep, grp = ("x", "z"), ("y", "core")
    placed = (
        P(None, rep + grp, None),
        P(None, rep + grp, None),
        P(None, grp, None),
        P(None, grp),
        P(rep, None, grp, None),
        P(None, grp, None),
        P(None, grp),
        P(),
    )

    return jax.shard_map(
        body,
        mesh=split,
        in_specs=placed,
        out_specs=(P(), P(), P(rep, None, grp, None), P(None, grp, None), P(None, grp)),
        check_vma=False,
    )
```

```python
import jax
import jax.numpy as jnp
from jax import lax
from jax.experimental import pallas as pl
from jax.experimental.pallas import tpu as pltpu
from jax.sharding import Mesh
from jax.sharding import PartitionSpec as P


NS_STEPS = 5
HIGH = lax.Precision.HIGHEST
BF = jnp.bfloat16
F32 = jnp.float32


def ring(count, step):
    return [(i, (i + step) % count) for i in range(count)]


def pick(stack, index, axis=0):
    return lax.dynamic_index_in_dim(stack, index, axis, keepdims=False)


def hi_lo(row):
    high = row.astype(BF)
    low = (row - high.astype(F32)).astype(BF)
    return jnp.concatenate([high[None], low[None], jnp.zeros((6, row.shape[0]), BF)], 0)


def from_hi_lo(rows):
    return rows[0].astype(F32) + rows[1].astype(F32)


def paired(parts):
    return (parts[0] + parts[2]) + (parts[1] + parts[3])


def split3(value):
    one = value.astype(BF)
    rest = value - one.astype(F32)
    two = rest.astype(BF)
    three = (rest - two.astype(F32)).astype(BF)
    return jnp.concatenate([one, two, three], 0)


def by_three(left, right, dims):
    rank = left.shape[0]
    out = lax.dot_general(split3(left), right, dims, preferred_element_type=F32)
    return out[:rank] + out[rank : 2 * rank] + out[2 * rank :]


def exact(left, right, dims):
    return lax.dot_general(left, right, dims, precision=HIGH, preferred_element_type=F32)


NN = (((1,), (0,)), ((), ()))
NT = (((1,), (1,)), ((), ()))
TN = (((0,), (0,)), ((), ()))


def inverse_root(gram):
    fro = jnp.sqrt(jnp.sum(gram * gram, axis=(0, 1), keepdims=True)) + 1e-06
    rank = gram.shape[0]
    spot = lambda axis: lax.broadcasted_iota(jnp.int32, (rank, rank), axis)
    eye = jnp.where(spot(0) == spot(1), 1.0, 0.0).astype(F32)

    def step(pair):
        ymat, zmat = pair
        tmat = 1.5 * eye - 0.5 * exact(zmat, ymat, NN)
        return exact(ymat, tmat, NN), exact(tmat, zmat, NN)

    pair = (gram / fro, eye)
    for _ in range(NS_STEPS):
        pair = step(pair)
    zmat = pair[1]
    return zmat, jnp.sqrt(fro)


def half_round(q, rows_of_sum):
    p = by_three(q, rows_of_sum, NT)
    return p, exact(p, p, NT), by_three(p, rows_of_sum, NN)


def store_split(ref, at, value):
    rank, wide = value.shape
    high = value.astype(BF)
    ref[:rank, at : at + wide] = high
    ref[:rank, at + wide : at + 2 * wide] = (value - high.astype(F32)).astype(BF)


def widened(gram):
    rank = gram.shape[0]
    return jnp.concatenate([gram, jnp.zeros((rank, 128 - rank), F32)], 1)


def first_kernel(xpos_ref, *refs):
    parts, (q_ref, bias_ref, sum_ref, out_ref) = refs[:4], refs[4:]
    rank, width = q_ref.shape
    piece = parts[0].shape[0]
    xpos = xpos_ref[0]
    for j in range(4):
        value = parts[j][...]
        for spot in (1, 2, 3):
            value = jnp.where(xpos == spot, parts[spot ^ j][...], value)
        sum_ref[j * piece : (j + 1) * piece] = value
    rest = sum_ref.shape[0] - 4 * piece
    sum_ref[4 * piece :] = jnp.zeros((rest, width), BF)
    _, gram, u = half_round(q_ref[...], sum_ref[...])
    out_ref[:rank, :width] = u.astype(BF)
    store_split(out_ref, width, widened(gram))
    bias = bias_ref[...]
    high = bias.astype(BF).astype(F32)
    both = jnp.concatenate([high, bias - high, jnp.zeros((6, width), F32)], 0)
    both = jnp.concatenate([both, jnp.zeros((8, 256), F32)], 1)
    out_ref[rank:] = both.astype(BF)


def sum_kernel(own_ref, own_bias_ref, *refs):
    parts, out_ref = refs[:3], refs[3]
    rows, width = own_ref.shape
    main = [own_ref[...]] + [part[:rows].astype(F32) for part in parts]
    tail = [own_bias_ref[...].astype(F32)] + [part[rows:].astype(F32) for part in parts]
    out_ref[:rows] = paired(main).astype(BF)
    bias = paired([t[:1] + t[1:2] for t in tail])
    high = bias.astype(BF).astype(F32)
    both = jnp.concatenate([high, bias - high, jnp.zeros((6, width), F32)], 0)
    out_ref[rows:] = both.astype(BF)


def summed_parts(parts, columns):
    load = lambda ref: ref[:, :columns].astype(F32)
    return (load(parts[0]) + load(parts[1])) + (load(parts[2]) + load(parts[3]))


def second_kernel(*refs):
    parts, (far_ref, out_ref, bias_ref, sum_ref, arrived) = refs[:4], refs[4:]
    fetch = pltpu.make_async_copy(far_ref, sum_ref, arrived)
    fetch.start()
    width = sum_ref.shape[1]
    rank = out_ref.shape[0]
    total = summed_parts(parts, width + 256)
    gram = total[:rank, width : width + 128] + total[:rank, width + 128 :]
    zmat, root = inverse_root(gram[:, :rank])
    q = exact(zmat, total[:rank, :width], TN) / root
    bias = total[rank : rank + 1, :width] + total[rank + 1 : rank + 2, :width]
    bias_ref[...] = jnp.concatenate([bias, jnp.zeros((7, width), F32)], 0)
    fetch.wait()
    p, gram, u = half_round(q, sum_ref[...])
    out_ref[:, :width] = u.astype(BF)
    store_split(out_ref, width, widened(gram))
    store_split(out_ref, width + 256, p)


def third_kernel(*refs):
    parts, (q_ref, z_ref) = refs[:4], refs[4:]
    rank, width = q_ref.shape
    total = summed_parts(parts, width + 256)
    gram = total[:, width : width + 128] + total[:, width + 128 :]
    zmat, root = inverse_root(gram[:, :rank])
    q_ref[...] = exact(zmat, total[:, :width], TN) / root
    z_ref[...] = zmat / root


def lineup_kernel(ypos_ref, *refs):
    parts, out_ref = refs[:4], refs[4]
    for spot in range(4):

        @pl.when(ypos_ref[0] == spot)
        def _():
            for j in range(4):
                out_ref[j] = parts[spot ^ j][...]


def lineup(ypos, parts):
    layers, held, width = parts[0].shape
    block = pl.BlockSpec((1, held, width), lambda i, ypos: (i, 0, 0))
    return pl.pallas_call(
        lineup_kernel,
        out_shape=jax.ShapeDtypeStruct((4, layers, held, width), BF),
        grid_spec=pltpu.PrefetchScalarGridSpec(
            num_scalar_prefetch=1,
            grid=(layers,),
            in_specs=[block] * 4,
            out_specs=pl.BlockSpec((4, 1, held, width), lambda i, ypos: (0, i, 0, 0)),
        ),
        name="lineup",
    )(ypos, *parts)


def assemble_kernel(core_ref, mine_ref, theirs_ref, out_ref):
    rows = out_ref.shape[1] // 2
    for spot in range(2):

        @pl.when(core_ref[0] == spot)
        def _():
            for side in range(2):
                ref = mine_ref if side == spot else theirs_ref
                out_ref[:, side * rows : (side + 1) * rows] = ref[0, :, :rows]


def assemble(core, mine, theirs, rows):
    ys, layers, held, width = mine.shape
    block = pl.BlockSpec((1, layers, held, width), lambda j, core: (j, 0, 0, 0))
    return pl.pallas_call(
        assemble_kernel,
        out_shape=jax.ShapeDtypeStruct((layers, width, width), BF),
        grid_spec=pltpu.PrefetchScalarGridSpec(
            num_scalar_prefetch=1,
            grid=(ys,),
            in_specs=[block, block],
            out_specs=pl.BlockSpec((layers, 2 * rows, width), lambda j, core: (0, j, 0)),
        ),
        name="assemble",
    )(core, mine, theirs)


def in_vmem(kernel, outs, scalars=0, far=0, scratch=()):
    vmem = pl.BlockSpec(memory_space=pltpu.VMEM)
    smem = pl.BlockSpec(memory_space=pltpu.SMEM)

    def call(*args):
        return pl.pallas_call(
            kernel,
            out_shape=outs,
            in_specs=[smem] * scalars
            + [vmem] * (len(args) - scalars - far)
            + [pl.BlockSpec(memory_space=pl.ANY)] * far,
            scratch_shapes=list(scratch),
            out_specs=jax.tree.map(lambda _: vmem, outs),
            compiler_params=pltpu.CompilerParams(vmem_limit_bytes=24 << 20),
        )(*args)

    return call


def products(left, right):
    l1 = left.astype(BF)
    rest = left - l1.astype(F32)
    l2 = rest.astype(BF)
    l3 = (rest - l2.astype(F32)).astype(BF)
    r1 = right.astype(BF)
    rest = right - r1.astype(F32)
    r2 = rest.astype(BF)
    r3 = (rest - r2.astype(F32)).astype(BF)
    return (
        jnp.concatenate([l1, l1, l2, l1, l2, l3], -2),
        jnp.concatenate([r1, r2, r1, r3, r2, r1], -2),
    )


def body(inputs, out_grads, weights, biases, errors, momenta, bias_momenta, q_start):
    layers, tok, width = inputs.shape
    cores = lax.axis_size("core")
    ys = lax.axis_size("y")
    xs = lax.axis_size("x")
    reps = xs * lax.axis_size("z")
    rows = width // (cores * ys)
    rank = q_start.shape[-1]
    scale = float(tok) ** (-0.5)
    core, ypos, xpos = lax.axis_index("core"), lax.axis_index("y"), lax.axis_index("x")

    def swap(value):
        return lax.ppermute(value, "core", ring(cores, 1))

    def trade(value, axis, k):
        return lax.ppermute(value, axis, [(i, i ^ k) for i in range(4)])

    def from_back(value, axis, k):
        return lax.ppermute(value, axis, ring(4, k))

    def everyone(value, axis):
        return [value] + [trade(value, axis, k) for k in (1, 2, 3)]

    def natural(parts, position):
        ordered = []
        for j in range(4):
            value = parts[j]
            for spot in (1, 2, 3):
                value = jnp.where(position == spot, parts[spot ^ j], value)
            ordered.append(value)
        return ordered

    old_m = lax.optimization_barrier(momenta)
    old = (weights.astype(F32) - 0.45 * old_m).astype(BF)
    row_b, row_m = lax.optimization_barrier((biases, bias_momenta))
    two = jnp.stack([row_b, row_m.astype(BF)], 1)
    old = jnp.concatenate([old, jnp.pad(two, ((0, 0), (0, 6), (0, width - rows)))], 1)
    parts = [old]
    for k in (1, 2, 3):
        parts.append(trade(old, "y", k))
    mine = lineup(ypos.astype(jnp.int32)[None], parts)
    theirs = swap(mine)
    old = assemble(core.astype(jnp.int32)[None], mine, theirs, rows)
    tail = mine[:, :, rows : rows + 2, :rows].astype(F32)
    tail = tail[:, :, 0] - 0.45 * tail[:, :, 1]
    even, odd = jnp.where(core == 0, tail, 0.0), jnp.where(core == 0, 0.0, tail)
    pieces = [side[j] for j in range(ys) for side in (even, odd)]
    half_b = jnp.concatenate(pieces, -1)

    def chip_blocks(layer, after=None):
        x, y = inputs, out_grads
        if after is not None:
            x, y, _ = lax.optimization_barrier((x, y, after))
        part = jnp.einsum("tr,te->re", x[layer], y[layer], preferred_element_type=F32).astype(BF)
        part = lax.optimization_barrier(part).reshape(ys * cores, rows, width)
        got = swap(
            pick(part.reshape(ys, cores, rows, width), 1 - core, 1)
        )
        keep = lax.optimization_barrier(pick(part.reshape(ys, cores, rows, width), core, 1))
        keep = keep if layer == 1 else pick(part.reshape(ys, cores, rows, width), core, 1)
        blocks = []
        for k in range(4):
            there = ypos ^ k
            blocks.append(pick(keep, there).astype(F32) + pick(got, there).astype(F32))
        return blocks[0], [b.astype(BF) for b in blocks[1:]]

    def merge(layer, own, blocks):
        for k in (1, 2, 3):
            block = trade(blocks[k - 1], "y", k)
            own = own + block.astype(F32)
        held = errors if layer else lax.optimization_barrier(errors)
        return own * scale + held[0, layer]

    own0, blocks0 = chip_blocks(0)
    own1, blocks1 = chip_blocks(1, blocks0)
    merged0 = lax.optimization_barrier(merge(0, own0, blocks0))
    merged = jnp.stack([merged0, merge(1, own1, blocks1)])
    col_sums = jnp.sum(out_grads, axis=1, dtype=F32)

    got = swap(
        jnp.concatenate([pick(merged, 1 - core).astype(BF), hi_lo(pick(col_sums, 1 - core))], 0)
    )
    own, got_rows = pick(merged, core), got[:rows].astype(F32)
    both = jnp.stack([jnp.where(core == 0, own, got_rows), jnp.where(core == 0, got_rows, own)])
    both = both.reshape(4, rows // 2, width)
    bias = pick(col_sums, core) + from_hi_lo(got[rows:])
    bias_rows = hi_lo(bias)
    half = rows // 2

    def loaded(main):
        return jnp.concatenate([main.astype(BF), bias_rows], 0)

    parts = []
    for k in (1, 2, 3):
        block = loaded(pick(both, (xpos + k) % 4))
        parts.append(from_back(block, "x", k))
    block = in_vmem(sum_kernel, jax.ShapeDtypeStruct((half + 8, width), BF))(
        pick(both, xpos), bias_rows, *parts
    )
    parts = [block] + [from_back(block, "z", k) for k in (1, 2, 3)]
    main = paired([p[:half].astype(F32) for p in parts]).astype(BF)
    bias = paired([from_hi_lo(p[half:]) for p in parts])
    parts = everyone(main, "x")
    shape = lambda *dims, of: jax.ShapeDtypeStruct(dims, of)
    q = pick(q_start, core).T
    total, packed = in_vmem(
        first_kernel, (shape(384, width, of=BF), shape(rank + 8, width + 256, of=BF)), 1
    )(xpos.astype(jnp.int32)[None], *parts, q, bias[None])
    parts = everyone(packed, "y")
    packed, bias_rows = in_vmem(
        second_kernel,
        (shape(rank, width + 1024, of=BF), shape(8, width, of=F32)),
        far=1,
        scratch=(pltpu.VMEM((384, width), BF), pltpu.SemaphoreType.DMA),
    )(*parts, total)
    parts = everyone(packed, "y")
    bias_rows = jnp.concatenate([bias_rows[:1], half_b, bias_rows[3:]], 0)
    other = swap(bias_rows)
    bias = jnp.stack([jnp.where(core == l, bias_rows[0], other[0]) for l in range(layers)])
    bias_grad = bias * (scale / reps)
    grp = ypos * cores + core
    bias_own = lax.dynamic_slice_in_dim(bias_grad, grp * rows, rows, 1)
    new_bias_momenta = 0.9 * bias_momenta + bias_own
    old_b = bias_rows[1:3] + other[1:3]
    new_biases = (old_b - 0.5 * bias_grad).astype(BF)
    q, zmat = in_vmem(third_kernel, (shape(rank, width, of=F32), shape(rank, rank, of=F32)))(*parts)
    at = width + 256
    p_all = [
        part[:, at : at + 2 * rows].astype(F32) + part[:, at + 384 : at + 384 + 2 * rows].astype(F32)
        for part in parts
    ]
    p_all = jnp.concatenate(natural(p_all, ypos), 1)
    phat = exact(zmat, p_all, TN)

    packed = jnp.concatenate([q, phat], 1)
    other = swap(packed)
    pair = [jnp.where(core == layer, packed, other) for layer in range(layers)]
    q = jnp.stack([p[:, :width] for p in pair])
    phat = jnp.stack([p[:, width:] for p in pair])
    left, right = products(phat, q)
    own = lax.dynamic_slice_in_dim(left, grp * rows, rows, 2)
    spec = "lkr,lke->lre"
    approx = jnp.einsum(spec, own, right, preferred_element_type=F32) * (1.0 / reps)
    new_errors = merged - approx
    new_momenta = 0.9 * momenta + approx
    whole = jnp.einsum(spec, left, right, preferred_element_type=F32) * (1.0 / reps)
    new_weights = (old.astype(F32) - 0.5 * whole).astype(BF)

    return (new_weights, new_biases, new_errors[None], new_momenta, new_bias_momenta)


def solution(mesh):
    split = Mesh(mesh.devices.reshape(4, 4, 4, 2), ("x", "z", "y", "core"))
    rep, grp = ("x", "z"), ("y", "core")
    placed = (
        P(None, rep + grp, None),
        P(None, rep + grp, None),
        P(None, grp, None),
        P(None, grp),
        P(rep, None, grp, None),
        P(None, grp, None),
        P(None, grp),
        P(),
    )

    return jax.shard_map(
        body,
        mesh=split,
        in_specs=placed,
        out_specs=(P(), P(), P(rep, None, grp, None), P(None, grp, None), P(None, grp)),
        check_vma=False,
    )
```

```python
import jax
import jax.numpy as jnp
from jax import lax
from jax.experimental import pallas as pl
from jax.experimental.pallas import tpu as pltpu
from jax.sharding import Mesh
from jax.sharding import PartitionSpec as P


NS_STEPS = 5
HIGH = lax.Precision.HIGHEST
BF = jnp.bfloat16
F32 = jnp.float32


def ring(count, step):
    return [(i, (i + step) % count) for i in range(count)]


def pick(stack, index, axis=0):
    return lax.dynamic_index_in_dim(stack, index, axis, keepdims=False)


def hi_lo(row):
    high = row.astype(BF)
    low = (row - high.astype(F32)).astype(BF)
    return jnp.concatenate([high[None], low[None], jnp.zeros((6, row.shape[0]), BF)], 0)


def from_hi_lo(rows):
    return rows[0].astype(F32) + rows[1].astype(F32)


def paired(parts):
    return (parts[0] + parts[2]) + (parts[1] + parts[3])


def split3(value):
    one = value.astype(BF)
    rest = value - one.astype(F32)
    two = rest.astype(BF)
    three = (rest - two.astype(F32)).astype(BF)
    return jnp.concatenate([one, two, three], 0)


def by_three(left, right, dims):
    rank = left.shape[0]
    out = lax.dot_general(split3(left), right, dims, preferred_element_type=F32)
    return out[:rank] + out[rank : 2 * rank] + out[2 * rank :]


def exact(left, right, dims):
    return lax.dot_general(left, right, dims, precision=HIGH, preferred_element_type=F32)


NN = (((1,), (0,)), ((), ()))
NT = (((1,), (1,)), ((), ()))
TN = (((0,), (0,)), ((), ()))


def inverse_root(gram):
    fro = jnp.sqrt(jnp.sum(gram * gram, axis=(0, 1), keepdims=True)) + 1e-06
    rank = gram.shape[0]
    spot = lambda axis: lax.broadcasted_iota(jnp.int32, (rank, rank), axis)
    eye = jnp.where(spot(0) == spot(1), 1.0, 0.0).astype(F32)

    def step(pair):
        ymat, zmat = pair
        tmat = 1.5 * eye - 0.5 * exact(zmat, ymat, NN)
        return exact(ymat, tmat, NN), exact(tmat, zmat, NN)

    pair = (gram / fro, eye)
    for _ in range(NS_STEPS):
        pair = step(pair)
    zmat = pair[1]
    return zmat, jnp.sqrt(fro)


def half_round(q, rows_of_sum):
    p = by_three(q, rows_of_sum, NT)
    return p, exact(p, p, NT), by_three(p, rows_of_sum, NN)


def store_split(ref, at, value):
    rank, wide = value.shape
    high = value.astype(BF)
    ref[:rank, at : at + wide] = high
    ref[:rank, at + wide : at + 2 * wide] = (value - high.astype(F32)).astype(BF)


def widened(gram):
    rank = gram.shape[0]
    return jnp.concatenate([gram, jnp.zeros((rank, 128 - rank), F32)], 1)


def first_kernel(xpos_ref, *refs):
    parts, (q_ref, bias_ref, sum_ref, out_ref) = refs[:4], refs[4:]
    rank, width = q_ref.shape
    piece = parts[0].shape[0]
    xpos = xpos_ref[0]
    for j in range(4):
        value = parts[j][...]
        for spot in (1, 2, 3):
            value = jnp.where(xpos == spot, parts[spot ^ j][...], value)
        sum_ref[j * piece : (j + 1) * piece] = value
    rest = sum_ref.shape[0] - 4 * piece
    sum_ref[4 * piece :] = jnp.zeros((rest, width), BF)
    _, gram, u = half_round(q_ref[...], sum_ref[...])
    out_ref[:rank, :width] = u.astype(BF)
    store_split(out_ref, width, widened(gram))
    bias = bias_ref[...]
    high = bias.astype(BF).astype(F32)
    both = jnp.concatenate([high, bias - high, jnp.zeros((6, width), F32)], 0)
    both = jnp.concatenate([both, jnp.zeros((8, 256), F32)], 1)
    out_ref[rank:] = both.astype(BF)


def summed_parts(parts, columns):
    load = lambda ref: ref[:, :columns].astype(F32)
    return (load(parts[0]) + load(parts[1])) + (load(parts[2]) + load(parts[3]))


def second_kernel(*refs):
    parts, (far_ref, out_ref, bias_ref, sum_ref, arrived) = refs[:4], refs[4:]
    fetch = pltpu.make_async_copy(far_ref, sum_ref, arrived)
    fetch.start()
    width = sum_ref.shape[1]
    rank = out_ref.shape[0]
    total = summed_parts(parts, width + 256)
    gram = total[:rank, width : width + 128] + total[:rank, width + 128 :]
    zmat, root = inverse_root(gram[:, :rank])
    q = exact(zmat, total[:rank, :width], TN) / root
    bias = total[rank : rank + 1, :width] + total[rank + 1 : rank + 2, :width]
    bias_ref[...] = jnp.concatenate([bias, jnp.zeros((7, width), F32)], 0)
    fetch.wait()
    p, gram, u = half_round(q, sum_ref[...])
    out_ref[:, :width] = u.astype(BF)
    store_split(out_ref, width, widened(gram))
    store_split(out_ref, width + 256, p)


def third_kernel(*refs):
    parts, (q_ref, z_ref) = refs[:4], refs[4:]
    rank, width = q_ref.shape
    total = summed_parts(parts, width + 256)
    gram = total[:, width : width + 128] + total[:, width + 128 :]
    zmat, root = inverse_root(gram[:, :rank])
    q_ref[...] = exact(zmat, total[:, :width], TN) / root
    z_ref[...] = zmat / root


def lineup_kernel(ypos_ref, *refs):
    parts, out_ref = refs[:4], refs[4]
    for spot in range(4):

        @pl.when(ypos_ref[0] == spot)
        def _():
            for j in range(4):
                out_ref[j] = parts[spot ^ j][...]


def lineup(ypos, parts):
    layers, held, width = parts[0].shape
    block = pl.BlockSpec((1, held, width), lambda i, ypos: (i, 0, 0))
    return pl.pallas_call(
        lineup_kernel,
        out_shape=jax.ShapeDtypeStruct((4, layers, held, width), BF),
        grid_spec=pltpu.PrefetchScalarGridSpec(
            num_scalar_prefetch=1,
            grid=(layers,),
            in_specs=[block] * 4,
            out_specs=pl.BlockSpec((4, 1, held, width), lambda i, ypos: (0, i, 0, 0)),
        ),
        name="lineup",
    )(ypos, *parts)


def assemble_kernel(core_ref, mine_ref, theirs_ref, out_ref):
    rows = out_ref.shape[1] // 2
    for spot in range(2):

        @pl.when(core_ref[0] == spot)
        def _():
            for side in range(2):
                ref = mine_ref if side == spot else theirs_ref
                out_ref[:, side * rows : (side + 1) * rows] = ref[0, :, :rows]


def assemble(core, mine, theirs, rows):
    ys, layers, held, width = mine.shape
    block = pl.BlockSpec((1, layers, held, width), lambda j, core: (j, 0, 0, 0))
    return pl.pallas_call(
        assemble_kernel,
        out_shape=jax.ShapeDtypeStruct((layers, width, width), BF),
        grid_spec=pltpu.PrefetchScalarGridSpec(
            num_scalar_prefetch=1,
            grid=(ys,),
            in_specs=[block, block],
            out_specs=pl.BlockSpec((layers, 2 * rows, width), lambda j, core: (0, j, 0)),
        ),
        name="assemble",
    )(core, mine, theirs)


def in_vmem(kernel, outs, scalars=0, far=0, scratch=()):
    vmem = pl.BlockSpec(memory_space=pltpu.VMEM)
    smem = pl.BlockSpec(memory_space=pltpu.SMEM)

    def call(*args):
        return pl.pallas_call(
            kernel,
            out_shape=outs,
            in_specs=[smem] * scalars
            + [vmem] * (len(args) - scalars - far)
            + [pl.BlockSpec(memory_space=pl.ANY)] * far,
            scratch_shapes=list(scratch),
            out_specs=jax.tree.map(lambda _: vmem, outs),
            compiler_params=pltpu.CompilerParams(vmem_limit_bytes=24 << 20),
        )(*args)

    return call


def products(left, right):
    l1 = left.astype(BF)
    rest = left - l1.astype(F32)
    l2 = rest.astype(BF)
    l3 = (rest - l2.astype(F32)).astype(BF)
    r1 = right.astype(BF)
    rest = right - r1.astype(F32)
    r2 = rest.astype(BF)
    r3 = (rest - r2.astype(F32)).astype(BF)
    return (
        jnp.concatenate([l1, l1, l2, l1, l2, l3], -2),
        jnp.concatenate([r1, r2, r1, r3, r2, r1], -2),
    )


def body(inputs, out_grads, weights, biases, errors, momenta, bias_momenta, q_start):
    layers, tok, width = inputs.shape
    cores = lax.axis_size("core")
    ys = lax.axis_size("y")
    xs = lax.axis_size("x")
    reps = xs * lax.axis_size("z")
    rows = width // (cores * ys)
    rank = q_start.shape[-1]
    scale = float(tok) ** (-0.5)
    core, ypos, xpos = lax.axis_index("core"), lax.axis_index("y"), lax.axis_index("x")

    def swap(value):
        return lax.ppermute(value, "core", ring(cores, 1))

    def trade(value, axis, k):
        return lax.ppermute(value, axis, [(i, i ^ k) for i in range(4)])

    def from_back(value, axis, k):
        return lax.ppermute(value, axis, ring(4, k))

    def everyone(value, axis):
        return [value] + [trade(value, axis, k) for k in (1, 2, 3)]

    def natural(parts, position):
        ordered = []
        for j in range(4):
            value = parts[j]
            for spot in (1, 2, 3):
                value = jnp.where(position == spot, parts[spot ^ j], value)
            ordered.append(value)
        return ordered

    old_m = lax.optimization_barrier(momenta)
    old = (weights.astype(F32) - 0.45 * old_m).astype(BF)
    row_b, row_m = lax.optimization_barrier((biases, bias_momenta))
    two = jnp.stack([row_b, row_m.astype(BF)], 1)
    old = jnp.concatenate([old, jnp.pad(two, ((0, 0), (0, 6), (0, width - rows)))], 1)
    parts = [old]
    for k in (1, 2, 3):
        parts.append(trade(old, "y", k))
    mine = lineup(ypos.astype(jnp.int32)[None], parts)
    theirs = swap(mine)
    old = assemble(core.astype(jnp.int32)[None], mine, theirs, rows)
    tail = mine[:, :, rows : rows + 2, :rows].astype(F32)
    tail = tail[:, :, 0] - 0.45 * tail[:, :, 1]
    even, odd = jnp.where(core == 0, tail, 0.0), jnp.where(core == 0, 0.0, tail)
    pieces = [side[j] for j in range(ys) for side in (even, odd)]
    half_b = jnp.concatenate(pieces, -1)

    def chip_blocks(layer, after=None):
        x, y = inputs, out_grads
        if after is not None:
            x, y, _ = lax.optimization_barrier((x, y, after))
        part = jnp.einsum("tr,te->re", x[layer], y[layer], preferred_element_type=F32).astype(BF)
        part = lax.optimization_barrier(part).reshape(ys * cores, rows, width)
        got = swap(
            pick(part.reshape(ys, cores, rows, width), 1 - core, 1)
        )
        blocks = []
        for k in range(4):
            there = ypos ^ k
            blocks.append(pick(part, there * cores + core).astype(F32) + pick(got, there).astype(F32))
        return blocks[0], [b.astype(BF) for b in blocks[1:]]

    def merge(layer, own, blocks):
        for k in (1, 2, 3):
            block = trade(blocks[k - 1], "y", k)
            own = own + block.astype(F32)
        held = errors if layer else lax.optimization_barrier(errors)
        return own * scale + held[0, layer]

    own0, blocks0 = chip_blocks(0)
    own1, blocks1 = chip_blocks(1, blocks0)
    merged0 = lax.optimization_barrier(merge(0, own0, blocks0))
    merged = jnp.stack([merged0, merge(1, own1, blocks1)])
    col_sums = jnp.sum(out_grads, axis=1, dtype=F32)

    got = swap(
        jnp.concatenate([pick(merged, 1 - core).astype(BF), hi_lo(pick(col_sums, 1 - core))], 0)
    )
    own, got_rows = pick(merged, core), got[:rows].astype(F32)
    both = jnp.stack([jnp.where(core == 0, own, got_rows), jnp.where(core == 0, got_rows, own)])
    both = both.reshape(4, rows // 2, width)
    bias = pick(col_sums, core) + from_hi_lo(got[rows:])
    bias_rows = hi_lo(bias)
    half = rows // 2

    def loaded(main):
        return jnp.concatenate([main.astype(BF), bias_rows], 0)

    parts = []
    for k in (1, 2, 3):
        block = loaded(pick(both, (xpos + k) % 4))
        parts.append(from_back(block, "x", k))
    main = paired([pick(both, xpos)] + [p[:half].astype(F32) for p in parts])
    bias = paired([from_hi_lo(p) for p in [bias_rows] + [p[half:] for p in parts]])
    bias_rows = hi_lo(bias)
    block = loaded(main)
    parts = [block]
    for k in (1, 2, 3):
        parts.append(from_back(block, "z", k))
    main = paired([p[:half].astype(F32) for p in parts]).astype(BF)
    bias = paired([from_hi_lo(p[half:]) for p in parts])
    parts = everyone(main, "x")
    shape = lambda *dims, of: jax.ShapeDtypeStruct(dims, of)
    q = pick(q_start, core).T
    total, packed = in_vmem(
        first_kernel, (shape(384, width, of=BF), shape(rank + 8, width + 256, of=BF)), 1
    )(xpos.astype(jnp.int32)[None], *parts, q, bias[None])
    parts = everyone(packed, "y")
    packed, bias_rows = in_vmem(
        second_kernel,
        (shape(rank, width + 1024, of=BF), shape(8, width, of=F32)),
        far=1,
        scratch=(pltpu.VMEM((384, width), BF), pltpu.SemaphoreType.DMA),
    )(*parts, total)
    parts = everyone(packed, "y")
    bias_rows = jnp.concatenate([bias_rows[:1], half_b, bias_rows[3:]], 0)
    other = swap(bias_rows)
    bias = jnp.stack([jnp.where(core == l, bias_rows[0], other[0]) for l in range(layers)])
    bias_grad = bias * (scale / reps)
    grp = ypos * cores + core
    bias_own = lax.dynamic_slice_in_dim(bias_grad, grp * rows, rows, 1)
    new_bias_momenta = 0.9 * bias_momenta + bias_own
    old_b = bias_rows[1:3] + other[1:3]
    new_biases = (old_b - 0.5 * bias_grad).astype(BF)
    q, zmat = in_vmem(third_kernel, (shape(rank, width, of=F32), shape(rank, rank, of=F32)))(*parts)
    at = width + 256
    p_all = [
        part[:, at : at + 2 * rows].astype(F32) + part[:, at + 384 : at + 384 + 2 * rows].astype(F32)
        for part in parts
    ]
    p_all = jnp.concatenate(natural(p_all, ypos), 1)
    phat = exact(zmat, p_all, TN)

    packed = jnp.concatenate([q, phat], 1)
    other = swap(packed)
    pair = [jnp.where(core == layer, packed, other) for layer in range(layers)]
    q = jnp.stack([p[:, :width] for p in pair])
    phat = jnp.stack([p[:, width:] for p in pair])
    left, right = products(phat, q)
    own = lax.dynamic_slice_in_dim(left, grp * rows, rows, 2)
    spec = "lkr,lke->lre"
    approx = jnp.einsum(spec, own, right, preferred_element_type=F32) * (1.0 / reps)
    new_errors = merged - approx
    new_momenta = 0.9 * momenta + approx
    whole = jnp.einsum(spec, left, right, preferred_element_type=F32) * (1.0 / reps)
    new_weights = (old.astype(F32) - 0.5 * whole).astype(BF)

    return (new_weights, new_biases, new_errors[None], new_momenta, new_bias_momenta)


def solution(mesh):
    split = Mesh(mesh.devices.reshape(4, 4, 4, 2), ("x", "z", "y", "core"))
    rep, grp = ("x", "z"), ("y", "core")
    placed = (
        P(None, rep + grp, None),
        P(None, rep + grp, None),
        P(None, grp, None),
        P(None, grp),
        P(rep, None, grp, None),
        P(None, grp, None),
        P(None, grp),
        P(),
    )

    return jax.shard_map(
        body,
        mesh=split,
        in_specs=placed,
        out_specs=(P(), P(), P(rep, None, grp, None), P(None, grp, None), P(None, grp)),
        check_vma=False,
    )
```
